256 devices in a mesh: group: 2 (over core), trow: 8 (over z_lo, y), tcol: 16 (over z_hi, x).
Axes of the slice: x: 4, y: 4, z: 8 (z_hi: 4, z_lo: 2; z = z_hi * 2 + z_lo), core: 2. Of those that a mesh axis runs over, the one named last changes fastest.
Arguments:
- displacement: float32 [3, 512, 128, 256], P(None, ('group', 'trow'), 'tcol'), may hold values from -6 to 6
- velocity: float32 [3, 512, 128, 256], P(None, ('group', 'trow'), 'tcol'), may hold values from -6 to 6
- stiffness: float32 [512, 128], P(('group', 'trow'), 'tcol'), may hold values from 4 to 12
- wet_position: float32 [3, 65536], P(None, ('group', 'trow', 'tcol')), may hold values from -6 to 6
- wet_normal: float32 [3, 65536], P(None, ('group', 'trow', 'tcol')), may hold values from -6 to 6
- wet_area: float32 [65536], P(('group', 'trow', 'tcol')), may hold values from 0.0078125 to 0.078125
- wet_map: int32 [65536], P(('group', 'trow', 'tcol')), may hold values from 0 to 255
Outputs:
- displacement_out: float32 [3, 512, 128, 256], P(None, ('group', 'trow'), 'tcol')
- velocity_out: float32 [3, 512, 128, 256], P(None, ('group', 'trow'), 'tcol')
The draws below stay inside these ranges and needn't reach their ends.
Inputs may be any that keep to these rules, and one draw needn't show every extreme that they name: Each wet point lies on the patch of nodes of the device that holds it: wet_map gives a * 8 + b for the node (a, b) of that patch.
All inputs are finite; a program needn't handle non-finite values.
Results may differ from the reference program's by a relative error of at most 0.0018.
Values may be sent and summed in bfloat16 or wider, within the bound.
No kernel may reach another device: no remote copies, remote signals or barrier semaphores. Data moves between devices by JAX's collectives and lax.ppermute only.
A program may use at most 128 MiB of HBM per device.

```python
import math
import jax
import jax.numpy as jnp
from jax import lax

LOADS = 64
LAYERS = 4
SUBSTEPS = 4
COUPLED = 2
WET_DEV = 256
PA = 32
PB = 8
NA = 512
NB = 128
W = 65536
N_TCOL = 16


def state_field(key, salt):
    key = jax.random.fold_in(key, salt)
    first_key = jax.random.fold_in(key, 0)
    shape = (3, NA, NB, LAYERS * LOADS)
    layer = lax.broadcasted_iota(jnp.int32, shape, 3) // LOADS
    inner = layer < LAYERS - 1
    base = jax.random.normal(first_key, shape, jnp.float32)
    values = base * jnp.where(inner, 2.5, 1.0).astype(jnp.float32)
    return jnp.clip(values, -6.0, 6.0).astype(jnp.float32)


def draw_displacement(key, part):
    return state_field(key, 7001)


def draw_velocity(key, part):
    return state_field(key, 7002)


def place_ends(result, rng, low, largest):
    shape = result.shape
    place = [jax.random.randint(jax.random.fold_in(rng, axis), (), 0, shape[axis]) for axis in range(len(shape))]
    result = result.at[tuple(place)].set(low)
    longest = shape.index(max(shape))
    place[longest] = (place[longest] + 1) % shape[longest]
    return result.at[tuple(place)].set(largest)


def levels(rng, extent, cuts, smallest, top_value):
    level, own = 1.0, jax.random.fold_in(rng, 6)
    for dim, blocks in cuts:
        draws = jnp.exp(jax.random.uniform(jax.random.fold_in(own, dim), (blocks,), jnp.float32, smallest / len(cuts), top_value / len(cuts)))
        level = level * jnp.repeat(draws, extent[dim] // blocks).reshape([-1 if axis == dim else 1 for axis in range(len(extent))])
    return level


def bell_draw(key, shape, deviation, reach, pieces=(), held_as=jnp.bfloat16):
    loudness = levels(key, shape, pieces, -0.22, 0.18) if pieces else 1.0
    values = jax.random.normal(key, shape, jnp.float32) * deviation * loudness
    return jnp.minimum(jnp.maximum(values, -reach), reach).astype(held_as)


def setup_inputs(seed: int = 0) -> dict:
    keys = jax.random.split(jax.random.key(seed), 8)
    displacement = draw_displacement(jax.random.fold_in(keys[7], 71), 0)
    velocity = draw_velocity(jax.random.fold_in(keys[7], 71), 0)
    stiffness = jnp.clip(jnp.exp(math.log(12.0) - 1.0986123 * jax.random.uniform(keys[2], (NA, NB), jnp.float32) ** levels(keys[2], (NA, NB), ((0, 16), (1, 16)), -0.2, 0.2)), 4.0, 12.0)
    wet_position = bell_draw(keys[3], (3, W), 1.0, 6.0, ((1, 256),), jnp.float32)
    wet_normal = bell_draw(keys[4], (3, W), 1.0, 6.0, ((1, 256),), jnp.float32)
    wet_area = jnp.clip(jnp.exp(math.log(0.078125) - 2.3025851 * jax.random.uniform(keys[5], (W,), jnp.float32) ** levels(keys[5], (W,), ((0, 256),), -0.2, 0.2)), 0.0078125, 0.078125)
    wet_map = place_ends(jax.random.randint(keys[6], (W,), 0, PA * PB), jax.random.fold_in(keys[6], 1), 0, (PA * PB) - 1).astype(jnp.int32)
    return dict(displacement=displacement, velocity=velocity, stiffness=stiffness, wet_position=wet_position, wet_normal=wet_normal, wet_area=wet_area, wet_map=wet_map)


SPHERE_AREA = 4.0 * math.pi
SMOOTHING = 0.1
TIME_STEP = 0.3
THICKNESS = 0.5
SPLINE_TAPS = (2.0 / 3.0, -1.0 / 12.0, -1.0 / 12.0, -1.0 / 6.0)

def spline_apply(padded, height, breadth, margin):
    middle = padded[:, margin:margin + height, margin:margin + breadth]
    summed = 2.0 * SPLINE_TAPS[0] * middle
    for offset in (1, 2, 3):
        along_rows = padded[:, margin + offset:margin + offset + height, margin:margin + breadth] + padded[:, margin - offset:margin - offset + height, margin:margin + breadth]
        along_cols = padded[:, margin:margin + height, margin + offset:margin + offset + breadth] + padded[:, margin:margin + height, margin - offset:margin - offset + breadth]
        summed = summed + SPLINE_TAPS[offset] * (along_rows + along_cols)
    return summed

def thickness_term(values, stride):
    above_layer = jnp.concatenate([values[..., stride:], values[..., -stride:]], axis=3)
    below_layer = jnp.concatenate([values[..., :stride], values[..., :-stride]], axis=3)
    return 2.0 * values - above_layer - below_layer

def advance(displacement, velocity, stiffness_grid, loading, in_plane):
    acceleration = -(stiffness_grid * in_plane) - THICKNESS * thickness_term(displacement, LOADS)
    outermost = acceleration[..., -LOADS:] + loading
    acceleration = jnp.concatenate([acceleration[..., :-LOADS], outermost], axis=3)
    velocity = velocity + TIME_STEP * acceleration
    displacement = displacement + TIME_STEP * velocity
    return (displacement, velocity)

def kernel_tile(position, normal, area, targets):
    delta_x = targets[0][None, :] - position[0][:, None]
    delta_y = targets[1][None, :] - position[1][:, None]
    delta_z = targets[2][None, :] - position[2][:, None]
    numerator = normal[0][:, None] * delta_x + normal[1][:, None] * delta_y + normal[2][:, None] * delta_z
    squared = delta_x * delta_x + delta_y * delta_y + delta_z * delta_z + SMOOTHING * SMOOTHING
    weighted = area[:, None] * numerator
    return (weighted / (SPHERE_AREA * squared * jnp.sqrt(squared))).astype(jnp.bfloat16)

def reference(displacement, velocity, stiffness, wet_position, wet_normal, wet_area, wet_map):
    wet_index = jnp.arange(W, dtype=jnp.int32)
    device = wet_index // WET_DEV
    node_row = device // N_TCOL * PA + wet_map // PB
    node_col = device % N_TCOL * PB + wet_map % PB
    node = (node_row * NB + node_col).astype(jnp.int32)
    block_size = math.gcd(W, 512)
    block_count = W // block_size
    target_blocks = wet_position.reshape(3, block_count, block_size).transpose(1, 0, 2)
    stiffness_grid = stiffness[None, :, :, None]
    for repeat in range(COUPLED):
        outer_layer = velocity[..., -LOADS:].reshape(3, NA * NB, LOADS)
        picked = jnp.take(outer_layer, node, axis=1)
        speeds = (wet_normal[0][:, None] * picked[0] + wet_normal[1][:, None] * picked[1] + wet_normal[2][:, None] * picked[2]).T
        speed_rounded = lax.optimization_barrier(speeds.astype(jnp.bfloat16)).astype(jnp.float32)

        def block_product(targets):
            tile = lax.optimization_barrier(kernel_tile(wet_position, wet_normal, wet_area, targets)).astype(jnp.float32)
            return jnp.dot(speed_rounded, tile, precision=lax.Precision.HIGHEST)
        products = lax.map(block_product, target_blocks)
        summed = products.transpose(1, 0, 2).reshape(LOADS, W)
        pressure = 0.5 * speeds + summed
        contribution = -(wet_normal[:, :, None] * pressure.T[None, :, :])
        loading = jnp.stack([jax.ops.segment_sum(contribution[component], node, num_segments=NA * NB) for component in range(3)])
        loading = loading.reshape(3, NA, NB, LOADS)

        def evolve(state):
            position_now, speed_now, force_now = state
            for substep in range(SUBSTEPS):
                padded = jnp.pad(position_now, ((0, 0), (3, 3), (3, 3), (0, 0)))
                in_plane = spline_apply(padded, NA, NB, 3)
                position_now, speed_now = advance(position_now, speed_now, stiffness_grid, force_now, in_plane)
            return (position_now, speed_now)
        displacement, velocity = lax.map(evolve, (displacement[:, None], velocity[:, None], loading[:, None]))
        displacement = displacement[:, 0]
        velocity = velocity[:, 0]
    return (displacement, velocity)
```

```python
import functools
import math

import jax
import jax.numpy as jnp
import numpy as np
from jax import lax
from jax.experimental import pallas as pl
from jax.experimental.pallas import tpu as pltpu
from jax.sharding import PartitionSpec as P

SUBSTEPS = 4
COUPLED = 2
N = 16
PTS = 256
PB = 8
LOADS = 64
QL = 4
HALO = 128
EXT = PTS + 2 * HALO
DT = 0.3
ROWS = ("group", "trow")
F32, BF16 = jnp.float32, jnp.bfloat16
VMEM_LIMIT = 56 << 20


def params(n=0):
    return pltpu.CompilerParams(vmem_limit_bytes=VMEM_LIMIT)


def split3(x):
    hi = x.astype(BF16).astype(F32)
    rest = x - hi
    mid = rest.astype(BF16).astype(F32)
    return hi, mid, (rest - mid).astype(BF16).astype(F32)


def pick_rows(values, onehot):
    rows = values.shape[0]
    parts = jnp.concatenate(split3(values), axis=0).astype(BF16)
    out = jnp.dot(parts, onehot, preferred_element_type=F32)
    return out[:rows] + out[rows : 2 * rows] + out[2 * rows :]


def node_onehot(map_row):
    nodes = lax.broadcasted_iota(jnp.int32, (PTS, PTS), 0).astype(F32)
    return jnp.where(nodes == map_row, 1.0, 0.0).astype(BF16)


def pack_kernel(d_ref, v_ref, st_ref, x_ref, sp_ref, acc_ref):
    k = pl.program_id(0)
    dt, vt = d_ref[0].T, v_ref[0].T
    for c in range(N):
        for l in range(4):
            rows = slice(l * LOADS + c * QL, l * LOADS + (c + 1) * QL)
            x_ref[c, 0, 0, l * QL : (l + 1) * QL, :] = dt[rows]
            x_ref[c, 1, 0, l * QL : (l + 1) * QL, :] = vt[rows]
    picked = pick_rows(vt[3 * LOADS :], node_onehot(st_ref[6:7]))
    term = picked * st_ref[pl.ds(3 + k, 1), :]

    @pl.when(k == 0)
    def _():
        acc_ref[...] = term

    @pl.when(k > 0)
    def _():
        acc_ref[...] += term

    sp_ref[...] = acc_ref[...].astype(BF16)


def pack(d, v, static):
    return pl.pallas_call(
        pack_kernel,
        grid=(3,),
        in_specs=[
            pl.BlockSpec((1, PTS, PTS), lambda k: (k, 0, 0)),
            pl.BlockSpec((1, PTS, PTS), lambda k: (k, 0, 0)),
            pl.BlockSpec((8, PTS), lambda k: (0, 0)),
        ],
        out_specs=[
            pl.BlockSpec((N, 2, 1, 16, PTS), lambda k: (0, 0, k, 0, 0)),
            pl.BlockSpec((LOADS, PTS), lambda k: (0, 0)),
        ],
        out_shape=[
            jax.ShapeDtypeStruct((N, 2, 3, 16, PTS), F32),
            jax.ShapeDtypeStruct((LOADS, PTS), BF16),
        ],
        scratch_shapes=[pltpu.VMEM((LOADS, PTS), F32)],
        compiler_params=params(),
        name="pack",
    )(d, v, static)


def unpack_kernel(x_ref, d_ref, v_ref, dt_ref, vt_ref):
    for c in range(N):
        for l in range(4):
            rows = slice(l * LOADS + c * QL, l * LOADS + (c + 1) * QL)
            dt_ref[rows, :] = x_ref[c, 0, 0, l * QL : (l + 1) * QL, :]
            vt_ref[rows, :] = x_ref[c, 1, 0, l * QL : (l + 1) * QL, :]
    d_ref[0] = dt_ref[...].T
    v_ref[0] = vt_ref[...].T


def unpack(x):
    return pl.pallas_call(
        unpack_kernel,
        grid=(3,),
        in_specs=[pl.BlockSpec((N, 2, 1, 16, PTS), lambda k: (0, 0, k, 0, 0))],
        out_specs=[pl.BlockSpec((1, PTS, PTS), lambda k: (k, 0, 0))] * 2,
        out_shape=[jax.ShapeDtypeStruct((3, PTS, PTS), F32)] * 2,
        scratch_shapes=[pltpu.VMEM((PTS, PTS), F32)] * 2,
        compiler_params=params(),
        name="unpack",
    )(x)


def feature_rows(parts, order, extra):
    rows = [parts[k][o] for k in range(3) for o in order] + extra
    rows = rows + [jnp.zeros_like(rows[0])] * (32 - len(rows))
    return jnp.concatenate(rows, axis=0)


SOURCE_ORDER = (0, 0, 0, 1, 1, 2)
TARGET_ORDER = (0, 1, 2, 0, 1, 0)
TB = 512


def build_kernel(src_ref, tgt_ref, sp_ref, k_ref, o_ref, fn_ref, fs_ref, mid_ref):
    @pl.when(pl.program_id(0) == 0)
    def _():
        for k in range(3):
            mid_ref[k : k + 1, :] = jnp.broadcast_to(jnp.mean(src_ref[:, k, :]).reshape(1, 1), (1, PTS))
        for j in range(N):
            p = [src_ref[j, k : k + 1, :] - mid_ref[k : k + 1, :] for k in range(3)]
            w = src_ref[j, 6:7, :] * (1.0 / (4.0 * math.pi))
            m = [src_ref[j, 3 + k : 4 + k, :] * w for k in range(3)]
            shift = -(m[0] * p[0] + m[1] * p[1] + m[2] * p[2])
            square = p[0] * p[0] + p[1] * p[1] + p[2] * p[2] + 0.01
            one = jnp.ones_like(shift)
            fn = feature_rows([split3(a) for a in m], SOURCE_ORDER, list(split3(shift)))
            fs = feature_rows([split3(-2.0 * a) for a in p], SOURCE_ORDER, list(split3(square)) + [one] * 3)
            at = slice(j * PTS, (j + 1) * PTS)
            fn_ref[at, :] = fn.T.astype(BF16)
            fs_ref[at, :] = fs.T.astype(BF16)

    blocks = []
    for b in range(TB // PTS):
        t = [tgt_ref[b, k : k + 1, :] - mid_ref[k : k + 1, :] for k in range(3)]
        square = t[0] * t[0] + t[1] * t[1] + t[2] * t[2]
        one = jnp.ones_like(square)
        blocks.append(feature_rows([split3(a) for a in t], TARGET_ORDER, [one] * 3 + list(split3(square))))
    g = jnp.concatenate(blocks, axis=1).astype(BF16)
    total = None
    for j in range(N):
        at = slice(j * PTS, (j + 1) * PTS)
        numerator = jnp.dot(fn_ref[at, :], g, preferred_element_type=F32)
        inverse = lax.rsqrt(jnp.dot(fs_ref[at, :], g, preferred_element_type=F32))
        tile = (numerator * inverse * (inverse * inverse)).astype(BF16)
        k_ref[at, :] = tile
        part = jnp.dot(sp_ref[j], tile, preferred_element_type=F32)
        total = part if total is None else total + part
    for c in range(N):
        o_ref[c] = total[c * QL : (c + 1) * QL]


def build(src, tgt, sp):
    points = N * PTS
    return pl.pallas_call(
        build_kernel,
        grid=(points // TB,),
        in_specs=[
            pl.BlockSpec((N, 8, PTS), lambda i: (0, 0, 0)),
            pl.BlockSpec((TB // PTS, 8, PTS), lambda i: (i, 0, 0)),
            pl.BlockSpec((N, LOADS, PTS), lambda i: (0, 0, 0)),
        ],
        out_specs=[
            pl.BlockSpec((points, TB), lambda i: (0, i)),
            pl.BlockSpec((N, QL, TB), lambda i: (0, 0, i)),
        ],
        out_shape=[
            jax.ShapeDtypeStruct((points, points), BF16),
            jax.ShapeDtypeStruct((N, QL, points), F32),
        ],
        scratch_shapes=[
            pltpu.VMEM((points, 32), BF16),
            pltpu.VMEM((points, 32), BF16),
            pltpu.VMEM((8, PTS), F32),
        ],
        compiler_params=params(),
        cost_estimate=pl.CostEstimate(flops=80 << 30, bytes_accessed=40 << 20, transcendentals=16 << 20),
        name="build",
    )(src, tgt, sp)


TB2 = 1024


def product_kernel(k_ref, sp_ref, o_ref):
    total = None
    for j in range(N):
        part = jnp.dot(sp_ref[j], k_ref[j * PTS : (j + 1) * PTS, :], preferred_element_type=F32)
        total = part if total is None else total + part
    for c in range(N):
        o_ref[c] = total[c * QL : (c + 1) * QL]


def product(kernel, sp):
    points = N * PTS
    return pl.pallas_call(
        product_kernel,
        grid=(points // TB2,),
        in_specs=[
            pl.BlockSpec((points, TB2), lambda i: (0, i)),
            pl.BlockSpec((N, LOADS, PTS), lambda i: (0, 0, 0)),
        ],
        out_specs=pl.BlockSpec((N, QL, TB2), lambda i: (0, 0, i)),
        out_shape=jax.ShapeDtypeStruct((N, QL, points), F32),
        compiler_params=params(),
        cost_estimate=pl.CostEstimate(flops=20 << 30, bytes_accessed=34 << 20, transcendentals=0),
        name="product",
    )(kernel, sp)


def patch_speeds(v_rows, static, onehot):
    picked = pick_rows(v_rows, onehot)
    return sum(static[3 + k : 4 + k] * picked[8 * k : 8 * k + 8] for k in range(3))


def first_kernel(x_ref, st_ref, s_ref, first_ref, last_ref):
    for c in range(N):
        static = st_ref[c]
        v_rows = jnp.concatenate([x_ref[c, 1, k, 8:16, :] for k in range(3)], axis=0)
        s_ref[c] = patch_speeds(v_rows, static, node_onehot(static[6:7]))[4:8]
        for which in range(2):
            for k in range(3):
                rows = slice((which * 3 + k) * 16, (which * 3 + k + 1) * 16)
                first_ref[c, rows, :] = x_ref[c, which, k, :, :HALO]
                last_ref[c, rows, :] = x_ref[c, which, k, :, PTS - HALO :]
        stiff = jnp.broadcast_to(static[7:8], (8, PTS))
        first_ref[c, 96:104, :] = stiff[:, :HALO]
        last_ref[c, 96:104, :] = stiff[:, PTS - HALO :]


def first(x, static):
    return pl.pallas_call(
        first_kernel,
        out_shape=[
            jax.ShapeDtypeStruct((N, QL, PTS), F32),
            jax.ShapeDtypeStruct((N, 104, HALO), F32),
            jax.ShapeDtypeStruct((N, 104, HALO), F32),
        ],
        compiler_params=params(),
        name="first",
    )(x, static)


def load_kernel(rec_ref, s_ref, st_ref, l_ref, first_ref, last_ref):
    for c in range(N):
        at = slice(c * PTS, (c + 1) * PTS)
        pressure = 0.5 * s_ref[c]
        for j in range(N):
            pressure = pressure + rec_ref[j, :, at].astype(F32)
        pressure = jnp.concatenate([jnp.zeros_like(pressure), pressure], axis=0)
        static = st_ref[c]
        parts = jnp.concatenate([-(static[3 + k : 4 + k] * pressure) for k in range(3)], axis=0)
        parts = jnp.concatenate(split3(parts), axis=0).astype(BF16)
        out = lax.dot_general(
            parts, node_onehot(static[6:7]), (((1,), (1,)), ((), ())), preferred_element_type=F32
        )
        loading = out[:24] + out[24:48] + out[48:]
        l_ref[c] = loading
        for k in range(3):
            first_ref[c, k] = loading[8 * k + 4 : 8 * k + 8, :HALO]
            last_ref[c, k] = loading[8 * k + 4 : 8 * k + 8, PTS - HALO :]


def loads(rec, speeds, static):
    return pl.pallas_call(
        load_kernel,
        out_shape=[
            jax.ShapeDtypeStruct((N, 24, PTS), F32),
            jax.ShapeDtypeStruct((N, 3, QL, HALO), F32),
            jax.ShapeDtypeStruct((N, 3, QL, HALO), F32),
        ],
        compiler_params=params(),
        name="loads",
    )(rec, speeds, static)


def stencil_matrices():
    taps = {0: -16.0, 1: 1.0, 2: 1.0, 3: 2.0}
    count = EXT // PB
    own = np.zeros((count, PB, count, PB), np.float32)
    left = np.zeros((PTS // PB, PB, PTS // PB, PB), np.float32)
    right = np.zeros_like(left)
    for a in range(count):
        for b in range(PB):
            own[a, b, a, b] = taps[0]
            for o in (1, 2, 3):
                for s in (o, -o):
                    if 0 <= a + s < count:
                        own[a + s, b, a, b] = taps[o]
                    if 0 <= b + s < PB:
                        own[a, b + s, a, b] = taps[o]
                    elif a < PTS // PB:
                        (left if s < 0 else right)[a, (b + s) % PB, a, b] = taps[o]
    return own.reshape(EXT, EXT), left.reshape(PTS, PTS), right.reshape(PTS, PTS)


GROUP = 4


def solid_kernel(last, *refs):
    (x_ref, lo_ref, hi_ref, slo_ref, shi_ref, l_ref, llo_ref, lhi_ref, st_ref, own_ref, left_ref, right_ref, *outs) = refs
    *outs, d_ref, v_ref, xp_ref, lx_ref, sx_ref = outs
    own = slice(HALO, HALO + PTS)
    xp_ref[0] = jnp.zeros_like(xp_ref[0])
    xp_ref[N + 1] = jnp.zeros_like(xp_ref[0])
    for c in range(N):
        for k in range(3):
            rows = slice(16 * k, 16 * k + 16)
            for ref, w in ((d_ref, 0), (v_ref, 1)):
                halo = slice(48 * w + 16 * k, 48 * w + 16 * k + 16)
                ref[c, rows, :HALO] = lo_ref[c, halo, :]
                ref[c, rows, own] = x_ref[c, w, k]
                ref[c, rows, HALO + PTS :] = hi_ref[c, halo, :]
            zero = jnp.zeros((4, HALO), F32)
            lx_ref[c, 8 * k : 8 * k + 8, :HALO] = jnp.concatenate([zero, llo_ref[c, k]], axis=0)
            lx_ref[c, 8 * k : 8 * k + 8, own] = l_ref[c, 8 * k : 8 * k + 8]
            lx_ref[c, 8 * k : 8 * k + 8, HALO + PTS :] = jnp.concatenate([zero, lhi_ref[c, k]], axis=0)
        sx_ref[c, :, :HALO] = slo_ref[c] * (1.0 / 12.0)
        sx_ref[c, :, own] = jnp.broadcast_to(st_ref[c, 7:8, :], (8, PTS)) * (1.0 / 12.0)
        sx_ref[c, :, HALO + PTS :] = shi_ref[c] * (1.0 / 12.0)
    layer = lax.rem(lax.broadcasted_iota(jnp.int32, (48, EXT), 0), 16)
    below_top, above_bottom = layer < 12, layer >= 4

    def substep(_, carry):
        for c in range(N):
            d = d_ref[c]
            hi = d.astype(BF16)
            xp_ref[c + 1, :48] = hi
            xp_ref[c + 1, 48:] = (d - hi.astype(F32)).astype(BF16)
        for g in range(0, N, GROUP):
            total = jnp.dot(
                xp_ref[g + 1 : g + 1 + GROUP].reshape(GROUP * 96, EXT), own_ref[...], preferred_element_type=F32
            )
            left = xp_ref[g : g + GROUP].reshape(GROUP * 96, EXT)
            right = xp_ref[g + 2 : g + 2 + GROUP].reshape(GROUP * 96, EXT)
            side = [
                jnp.dot(left[:, h * PTS : (h + 1) * PTS], left_ref[...], preferred_element_type=F32)
                + jnp.dot(right[:, h * PTS : (h + 1) * PTS], right_ref[...], preferred_element_type=F32)
                for h in range(2)
            ]
            total = total + jnp.concatenate(side, axis=1)
            for i in range(GROUP):
                c = g + i
                y = total[96 * i : 96 * i + 48] + total[96 * i + 48 : 96 * i + 96]
                d = d_ref[c]
                thick = jnp.where(below_top, d - pltpu.roll(d, 44, 0), 0.0) + jnp.where(
                    above_bottom, d - pltpu.roll(d, 4, 0), 0.0
                )
                zero = jnp.zeros((8, EXT), F32)
                load = jnp.concatenate(
                    [a for k in range(3) for a in (zero, lx_ref[c, 8 * k : 8 * k + 8])], axis=0
                )
                stiff = jnp.concatenate([sx_ref[c]] * 6, axis=0)
                v = v_ref[c] + DT * (stiff * y - 0.5 * thick + load)
                v_ref[c] = v
                d_ref[c] = d + DT * v
        return carry

    lax.fori_loop(0, SUBSTEPS, substep, 0)
    for c in range(N):
        for k in range(3):
            rows = slice(16 * k, 16 * k + 16)
            for ref, w in ((d_ref, 0), (v_ref, 1)):
                outs[0][c, w, k] = ref[c, rows, own]
                if not last:
                    halo = slice(48 * w + 16 * k, 48 * w + 16 * k + 16)
                    outs[1][c, halo, :] = ref[c, rows, HALO : 2 * HALO]
                    outs[2][c, halo, :] = ref[c, rows, PTS : PTS + HALO]
        if not last:
            static = st_ref[c]
            v_rows = jnp.concatenate([v_ref[c, 16 * k + 8 : 16 * k + 16, own] for k in range(3)], axis=0)
            speeds = patch_speeds(v_rows, static, node_onehot(static[6:7]))[4:8]
            outs[3][c] = speeds
            outs[4][c] = speeds.astype(BF16)


def solid(last, x, lo, hi, first_lo, first_hi, loading, load_lo, load_hi, static, matrices):


    whole = pl.BlockSpec(memory_space=pltpu.VMEM)

    def full(a):
        return pl.BlockSpec(a.shape, lambda i: (0,) * a.ndim)

    halo = pl.BlockSpec((N, 96, HALO), lambda i: (0, 0, 0))
    stiff = pl.BlockSpec((N, 8, HALO), lambda i: (0, 12, 0))
    outs = [jax.ShapeDtypeStruct((N, 2, 3, 16, PTS), F32)]
    if not last:
        outs += [jax.ShapeDtypeStruct((N, 96, HALO), F32)] * 2
        outs += [jax.ShapeDtypeStruct((N, QL, PTS), F32), jax.ShapeDtypeStruct((N, QL, PTS), BF16)]
    return pl.pallas_call(
        functools.partial(solid_kernel, last),
        grid=(1,),
        in_specs=[full(x), halo, halo, stiff, stiff]
        + [full(a) for a in (loading, load_lo, load_hi, static, *matrices)],
        out_specs=[full(o) for o in outs],
        out_shape=outs,
        scratch_shapes=[
            pltpu.VMEM((N, 48, EXT), F32),
            pltpu.VMEM((N, 48, EXT), F32),
            pltpu.VMEM((N + 2, 96, EXT), BF16),
            pltpu.VMEM((N, 24, EXT), F32),
            pltpu.VMEM((N, 8, EXT), F32),
        ],
        compiler_params=params(),
        name="solid_last" if last else "solid",
    )(x, lo, hi, first_lo, first_hi, loading, load_lo, load_hi, static, *matrices)


def exchange(blocks, axis):
    return lax.all_to_all(blocks, axis, split_axis=0, concat_axis=0, tiled=True)


def copies(array, axis):
    return exchange(jnp.broadcast_to(array, (N, *array.shape)), axis)


def from_neighbours(first_rows, last_rows):
    down = [(i, i + 1) for i in range(N - 1)]
    up = [(b, a) for a, b in down]
    return lax.ppermute(last_rows, ROWS, down), lax.ppermute(first_rows, ROWS, up)


def on_device(displacement, velocity, stiffness, wet_position, wet_normal, wet_area, wet_map):
    shape = displacement.shape
    map_row = wet_map.astype(F32)[None]
    static_own = jnp.concatenate([wet_position, wet_normal, map_row, stiffness.reshape(1, PTS)], axis=0)
    source_own = jnp.concatenate([wet_position, wet_normal, wet_area[None], wet_area[None]], axis=0)
    src = copies(source_own, ROWS)
    static = copies(static_own, "tcol")
    blocks, speeds_own = pack(
        displacement.reshape(3, PTS, PTS), velocity.reshape(3, PTS, PTS), static_own
    )
    gathered = copies(speeds_own, ROWS)
    x = exchange(blocks, "tcol")
    kernel, partial = build(src, static, gathered)
    speeds, x_first, x_last = first(x, static)
    lo, hi = from_neighbours(x_first, x_last)
    first_lo, first_hi = lo, hi
    matrices = tuple(jnp.asarray(m, BF16) for m in stencil_matrices())
    for repeat in range(COUPLED):
        received = exchange(partial, "tcol")
        loading, load_first, load_last = loads(received, speeds, static)
        load_lo, load_hi = from_neighbours(load_first, load_last)
        last = repeat == COUPLED - 1
        x, *more = solid(last, x, lo, hi, first_lo, first_hi, loading, load_lo, load_hi, static, matrices)
        if last:
            break
        x_first, x_last, speeds, rounded = more
        own = exchange(rounded, "tcol").reshape(LOADS, PTS)
        gathered = copies(own, ROWS)
        lo, hi = from_neighbours(x_first, x_last)
        partial = product(kernel, gathered)
    d, v = unpack(exchange(x, "tcol"))
    return d.reshape(shape), v.reshape(shape)


def solution(mesh):
    state = P(None, ("group", "trow"), "tcol", None)
    points = P(("group", "trow", "tcol"))
    vectors = P(None, ("group", "trow", "tcol"))
    return jax.shard_map(
        on_device,
        mesh=mesh,
        in_specs=(state, state, P(("group", "trow"), "tcol"), vectors, vectors, points, points),
        out_specs=(state, state),
        check_vma=False,
    )
```

```python
import functools
import math

import jax
import jax.numpy as jnp
import numpy as np
from jax import lax
from jax.experimental import pallas as pl
from jax.experimental.pallas import tpu as pltpu
from jax.sharding import PartitionSpec as P

SUBSTEPS = 4
COUPLED = 2
N = 16
PTS = 256
PB = 8
LOADS = 64
SRC = LOADS + 32
QL = 4
HALO = 128
EXT = PTS + 2 * HALO
DT = 0.3
ROWS = ("group", "trow")
F32, BF16 = jnp.float32, jnp.bfloat16


def params(mib):
    return pltpu.CompilerParams(vmem_limit_bytes=mib << 20)


def split3(x):
    hi = x.astype(BF16).astype(F32)
    rest = x - hi
    mid = rest.astype(BF16).astype(F32)
    return hi, mid, (rest - mid).astype(BF16).astype(F32)


def encode(x):
    top = jnp.max(jnp.max(jnp.abs(x), axis=0, keepdims=True), axis=1, keepdims=True)
    exponent = jnp.floor(jnp.log2(jnp.maximum(top, 1e-30))) + 1.0
    scaled = jnp.round(x * jnp.exp2(15.0 - exponent))
    return jnp.clip(scaled, -32767.0, 32767.0), exponent


def to_i16(x):
    return x.astype(jnp.int32).astype(jnp.int16)


def from_i16(x):
    return x.astype(jnp.int32).astype(F32)


def encode_rows(ref, c, unit, x):
    low, e0 = encode(x[:8])
    high, e1 = encode(x[8:])
    ref[c, 16 * unit : 16 * unit + 16, :] = to_i16(jnp.concatenate([low, high], axis=0))
    return [jnp.broadcast_to(e, (1, PTS)) for e in (e0, e1)]


def decode_scales(ref, c):
    return jnp.exp2(from_i16(ref[c, 96:112, :]) - 15.0)


def decode_rows(ref, c, unit, scales):
    x = from_i16(ref[c, 16 * unit : 16 * unit + 16, :])
    return jnp.concatenate(
        [x[8 * h : 8 * h + 8] * scales[2 * unit + h : 2 * unit + h + 1] for h in range(2)], axis=0
    )


def pick_rows(values, onehot):
    rows = values.shape[0]
    parts = jnp.concatenate(split3(values), axis=0).astype(BF16)
    out = jnp.dot(parts, onehot, preferred_element_type=F32)
    return out[:rows] + out[rows : 2 * rows] + out[2 * rows :]


def node_onehot(map_row):
    nodes = lax.broadcasted_iota(jnp.int32, (PTS, PTS), 0).astype(F32)
    return jnp.where(nodes == map_row, 1.0, 0.0).astype(BF16)


def pack_kernel(d_ref, v_ref, st_ref, so_ref, x_ref, sp_ref, acc_ref):
    k = pl.program_id(0)
    dt, vt = d_ref[0].T, v_ref[0].T
    for c in range(N):
        for l in range(4):
            rows = slice(l * LOADS + c * QL, l * LOADS + (c + 1) * QL)
            x_ref[c, 0, 0, l * QL : (l + 1) * QL, :] = dt[rows]
            x_ref[c, 1, 0, l * QL : (l + 1) * QL, :] = vt[rows]
    picked = pick_rows(vt[3 * LOADS :], node_onehot(st_ref[6:7]))
    term = picked * st_ref[pl.ds(3 + k, 1), :]

    @pl.when(k == 0)
    def _():
        acc_ref[...] = term

    @pl.when(k > 0)
    def _():
        acc_ref[...] += term

    geometry = list(split3(so_ref[...]))
    sp_ref[...] = jnp.concatenate([acc_ref[...]] + geometry + geometry[2:], axis=0).astype(BF16)


def pack(d, v, static, source):
    return pl.pallas_call(
        pack_kernel,
        grid=(3,),
        in_specs=[
            pl.BlockSpec((1, PTS, PTS), lambda k: (k, 0, 0)),
            pl.BlockSpec((1, PTS, PTS), lambda k: (k, 0, 0)),
            pl.BlockSpec((8, PTS), lambda k: (0, 0)),
            pl.BlockSpec((8, PTS), lambda k: (0, 0)),
        ],
        out_specs=[
            pl.BlockSpec((N, 2, 1, 16, PTS), lambda k: (0, 0, k, 0, 0)),
            pl.BlockSpec((SRC, PTS), lambda k: (0, 0)),
        ],
        out_shape=[
            jax.ShapeDtypeStruct((N, 2, 3, 16, PTS), F32),
            jax.ShapeDtypeStruct((SRC, PTS), BF16),
        ],
        scratch_shapes=[pltpu.VMEM((LOADS, PTS), F32)],
        compiler_params=params(16),
        name="pack",
    )(d, v, static, source)


def unpack_kernel(x_ref, d_ref, v_ref, t_ref):
    for c in range(N):
        scales = decode_scales(x_ref, c)
        for unit in range(6):
            rows = decode_rows(x_ref, c, unit, scales)
            for l in range(4):
                at = slice(l * LOADS + c * QL, l * LOADS + (c + 1) * QL)
                t_ref[unit, at, :] = rows[l * QL : (l + 1) * QL]
    for k in range(3):
        d_ref[k] = t_ref[k].T
        v_ref[k] = t_ref[3 + k].T


def unpack(x):
    return pl.pallas_call(
        unpack_kernel,
        out_shape=[jax.ShapeDtypeStruct((3, PTS, PTS), F32)] * 2,
        scratch_shapes=[pltpu.VMEM((6, PTS, PTS), F32)],
        compiler_params=params(16),
        name="unpack",
    )(x)


def feature_rows(parts, order, extra):
    rows = [parts[k][o] for k in range(3) for o in order] + extra
    rows = rows + [jnp.zeros_like(rows[0])] * (32 - len(rows))
    return jnp.concatenate(rows, axis=0)


SOURCE_ORDER = (0, 0, 0, 1, 1, 2)
TARGET_ORDER = (0, 1, 2, 0, 1, 0)
TB = 512


def build_kernel(src_ref, tgt_ref, k_ref, o_ref, fn_ref, fs_ref, sp_ref, mid_ref, e_ref):

    @pl.when(pl.program_id(0) == 0)
    def _():
        total = None
        for j in range(N):
            sp_ref[j * PTS : (j + 1) * PTS, :] = src_ref[j, :LOADS, :].T
            geometry = src_ref[j, LOADS:, :].astype(F32)
            geometry = geometry[:8] + geometry[8:16] + geometry[16:24]
            total = geometry if total is None else total + geometry
        mid_ref[...] = jnp.broadcast_to(jnp.sum(total, axis=1, keepdims=True) * (1.0 / (N * PTS)), (8, PTS))
        for j in range(N):
            geometry = src_ref[j, LOADS:, :].astype(F32)
            geometry = geometry[:8] + geometry[8:16] + geometry[16:24]
            p = [geometry[k : k + 1] - mid_ref[k : k + 1, :] for k in range(3)]
            w = geometry[6:7] * (1.0 / (4.0 * math.pi))
            m = [geometry[3 + k : 4 + k] * w for k in range(3)]
            shift = -(m[0] * p[0] + m[1] * p[1] + m[2] * p[2])
            square = p[0] * p[0] + p[1] * p[1] + p[2] * p[2] + 0.01
            one = jnp.ones_like(shift)
            fn = feature_rows([split3(a) for a in m], SOURCE_ORDER, list(split3(shift)))
            fs = feature_rows([split3(-2.0 * a) for a in p], SOURCE_ORDER, list(split3(square)) + [one] * 3)
            at = slice(j * PTS, (j + 1) * PTS)
            fn_ref[:, at] = fn.astype(BF16)
            fs_ref[:, at] = fs.astype(BF16)

    for b in range(TB // PTS):
        t = [tgt_ref[b, k : k + 1, :] - mid_ref[k : k + 1, :] for k in range(3)]
        square = t[0] * t[0] + t[1] * t[1] + t[2] * t[2]
        one = jnp.ones_like(square)
        g = feature_rows([split3(a) for a in t], TARGET_ORDER, [one] * 3 + list(split3(square))).T.astype(BF16)
        for j in range(N):
            at = slice(j * PTS, (j + 1) * PTS)
            numerator = jnp.dot(g, fn_ref[:, at], preferred_element_type=F32)
            inverse = lax.rsqrt(jnp.dot(g, fs_ref[:, at], preferred_element_type=F32))
            k_ref[b * PTS : (b + 1) * PTS, at] = (numerator * inverse * (inverse * inverse)).astype(BF16)
    total = jnp.dot(k_ref[...], sp_ref[...], preferred_element_type=F32).T
    write_partial(total, o_ref, e_ref)


def write_partial(total, o_ref, e_ref):
    step = pl.program_id(0)
    width = total.shape[1]
    lane = lax.broadcasted_iota(jnp.int32, (LOADS, 128), 1)
    for b in range(width // TB):
        part = total[:, b * TB : (b + 1) * TB]
        top = jnp.max(jnp.abs(part), axis=1, keepdims=True)
        exponent = jnp.floor(jnp.log2(jnp.maximum(top, 1e-30))) + 1.0
        part = to_i16(jnp.clip(jnp.round(part * jnp.exp2(15.0 - exponent)), -32767.0, 32767.0))
        at = pl.ds(pl.multiple_of(step * width + b * TB, TB), TB)
        for c in range(N):
            o_ref[c, :, at] = part[c * QL : (c + 1) * QL]
        index = step * (width // TB) + b
        e_ref[...] = jnp.where(lane == index, exponent, jnp.where(index == 0, 0.0, e_ref[...]))

    @pl.when(step == pl.num_programs(0) - 1)
    def _():
        exponents = to_i16(e_ref[...])
        for c in range(N):
            o_ref[c, :, N * PTS :] = exponents[c * QL : (c + 1) * QL]


def build(src, tgt):
    points = N * PTS
    return pl.pallas_call(
        build_kernel,
        grid=(points // TB,),
        in_specs=[
            pl.BlockSpec((N, SRC, PTS), lambda i: (0, 0, 0)),
            pl.BlockSpec((TB // PTS, 8, PTS), lambda i: (i, 0, 0)),
        ],
        out_specs=[
            pl.BlockSpec((TB, points), lambda i: (i, 0)),
            pl.BlockSpec((N, QL, points + 128), lambda i: (0, 0, 0)),
        ],
        out_shape=[
            jax.ShapeDtypeStruct((points, points), BF16),
            jax.ShapeDtypeStruct((N, QL, points + 128), jnp.int16),
        ],
        scratch_shapes=[
            pltpu.VMEM((32, points), BF16),
            pltpu.VMEM((32, points), BF16),
            pltpu.VMEM((points, LOADS), BF16),
            pltpu.VMEM((8, PTS), F32),
            pltpu.VMEM((LOADS, 128), F32),
        ],
        compiler_params=params(24),
        cost_estimate=pl.CostEstimate(flops=20 << 30, bytes_accessed=100 << 20, transcendentals=16 << 20),
        name="build",
    )(src, tgt)


TB2 = 1024


def product_kernel(k_ref, own_ref, o_ref, sp_ref, e_ref):
    @pl.when(pl.program_id(0) == 0)
    def _():
        for j in range(N):
            sp_ref[j * PTS : (j + 1) * PTS, :] = own_ref[j].T

    total = jnp.dot(k_ref[...], sp_ref[...], preferred_element_type=F32).T
    write_partial(total, o_ref, e_ref)


def product(kernel, sp):
    points = N * PTS
    return pl.pallas_call(
        product_kernel,
        grid=(points // TB2,),
        in_specs=[
            pl.BlockSpec((TB2, points), lambda i: (i, 0)),
            pl.BlockSpec((N, LOADS, PTS), lambda i: (0, 0, 0)),
        ],
        out_specs=pl.BlockSpec((N, QL, points + 128), lambda i: (0, 0, 0)),
        out_shape=jax.ShapeDtypeStruct((N, QL, points + 128), jnp.int16),
        scratch_shapes=[pltpu.VMEM((points, LOADS), BF16), pltpu.VMEM((LOADS, 128), F32)],
        compiler_params=params(24),
        cost_estimate=pl.CostEstimate(flops=4 << 30, bytes_accessed=40 << 20, transcendentals=0),
        name="product",
    )(kernel, sp)


def patch_speeds(v_rows, static, onehot):
    picked = pick_rows(v_rows, onehot)
    return sum(static[3 + k : 4 + k] * picked[8 * k : 8 * k + 8] for k in range(3))


def first_kernel(x_ref, st_ref, s_ref, first_ref, last_ref):
    for c in range(N):
        static = st_ref[c]
        v_rows = jnp.concatenate([x_ref[c, 1, k, 8:16, :] for k in range(3)], axis=0)
        s_ref[c] = patch_speeds(v_rows, static, node_onehot(static[6:7]))[4:8]
        for which in range(2):
            for k in range(3):
                rows = slice((which * 3 + k) * 16, (which * 3 + k + 1) * 16)
                first_ref[c, rows, :] = x_ref[c, which, k, :, :HALO]
                last_ref[c, rows, :] = x_ref[c, which, k, :, PTS - HALO :]
        stiff = jnp.broadcast_to(static[7:8], (8, PTS))
        first_ref[c, 96:104, :] = stiff[:, :HALO]
        last_ref[c, 96:104, :] = stiff[:, PTS - HALO :]


def first(x, static):
    return pl.pallas_call(
        first_kernel,
        out_shape=[
            jax.ShapeDtypeStruct((N, QL, PTS), F32),
            jax.ShapeDtypeStruct((N, 104, HALO), F32),
            jax.ShapeDtypeStruct((N, 104, HALO), F32),
        ],
        compiler_params=params(20),
        name="first",
    )(x, static)


def load_kernel(rec_ref, s_ref, st_ref, l_ref, first_ref, last_ref):
    scales = [jnp.exp2(from_i16(rec_ref[j, :, N * PTS :]) - 15.0) for j in range(N)]
    for c in range(N):
        at = slice(c * PTS, (c + 1) * PTS)
        index = c * PTS // TB
        pressure = 0.5 * s_ref[c]
        for j in range(N):
            pressure = pressure + from_i16(rec_ref[j, :, at]) * scales[j][:, index : index + 1]
        pressure = jnp.concatenate([jnp.zeros_like(pressure), pressure], axis=0)
        static = st_ref[c]
        parts = jnp.concatenate([-(static[3 + k : 4 + k] * pressure) for k in range(3)], axis=0)
        parts = jnp.concatenate(split3(parts), axis=0).astype(BF16)
        out = lax.dot_general(
            parts, node_onehot(static[6:7]), (((1,), (1,)), ((), ())), preferred_element_type=F32
        )
        loading = out[:24] + out[24:48] + out[48:]
        l_ref[c] = loading
        for k in range(3):
            first_ref[c, k] = loading[8 * k + 4 : 8 * k + 8, :HALO]
            last_ref[c, k] = loading[8 * k + 4 : 8 * k + 8, PTS - HALO :]


def loads(rec, speeds, static):
    return pl.pallas_call(
        load_kernel,
        out_shape=[
            jax.ShapeDtypeStruct((N, 24, PTS), F32),
            jax.ShapeDtypeStruct((N, 3, QL, HALO), F32),
            jax.ShapeDtypeStruct((N, 3, QL, HALO), F32),
        ],
        compiler_params=params(20),
        name="loads",
    )(rec, speeds, static)


def stencil_matrices():
    taps = {0: -16.0, 1: 1.0, 2: 1.0, 3: 2.0}
    count = EXT // PB
    own = np.zeros((count, PB, count, PB), np.float32)
    left = np.zeros((PTS // PB, PB, PTS // PB, PB), np.float32)
    right = np.zeros_like(left)
    for a in range(count):
        for b in range(PB):
            own[a, b, a, b] = taps[0]
            for o in (1, 2, 3):
                for s in (o, -o):
                    if 0 <= a + s < count:
                        own[a + s, b, a, b] = taps[o]
                    if 0 <= b + s < PB:
                        own[a, b + s, a, b] = taps[o]
                    elif a < PTS // PB:
                        (left if s < 0 else right)[a, (b + s) % PB, a, b] = taps[o]
    return own.reshape(EXT, EXT), left.reshape(PTS, PTS), right.reshape(PTS, PTS)


GROUP = 4


def solid_kernel(last, *refs):
    (x_ref, lo_ref, hi_ref, slo_ref, shi_ref, l_ref, llo_ref, lhi_ref, st_ref, own_ref, left_ref, right_ref, *outs) = refs
    *outs, d_ref, v_ref, xp_ref, lx_ref, sx_ref = outs
    own = slice(HALO, HALO + PTS)
    xp_ref[0] = jnp.zeros_like(xp_ref[0])
    xp_ref[N + 1] = jnp.zeros_like(xp_ref[0])
    for c in range(N):
        for k in range(3):
            rows = slice(16 * k, 16 * k + 16)
            for ref, w in ((d_ref, 0), (v_ref, 1)):
                halo = slice(48 * w + 16 * k, 48 * w + 16 * k + 16)
                ref[c, rows, :HALO] = lo_ref[c, halo, :]
                ref[c, rows, own] = x_ref[c, w, k]
                ref[c, rows, HALO + PTS :] = hi_ref[c, halo, :]
            zero = jnp.zeros((4, HALO), F32)
            lx_ref[c, 8 * k : 8 * k + 8, :HALO] = jnp.concatenate([zero, llo_ref[c, k]], axis=0)
            lx_ref[c, 8 * k : 8 * k + 8, own] = l_ref[c, 8 * k : 8 * k + 8]
            lx_ref[c, 8 * k : 8 * k + 8, HALO + PTS :] = jnp.concatenate([zero, lhi_ref[c, k]], axis=0)
        sx_ref[c, :, :HALO] = slo_ref[c] * (1.0 / 12.0)
        sx_ref[c, :, own] = jnp.broadcast_to(st_ref[c, 7:8, :], (8, PTS)) * (1.0 / 12.0)
        sx_ref[c, :, HALO + PTS :] = shi_ref[c] * (1.0 / 12.0)
    layer = lax.rem(lax.broadcasted_iota(jnp.int32, (48, EXT), 0), 16)
    below_top, above_bottom = layer < 12, layer >= 4

    def substep(_, carry):
        for c in range(N):
            d = d_ref[c]
            hi = d.astype(BF16)
            xp_ref[c + 1, :48] = hi
            xp_ref[c + 1, 48:] = (d - hi.astype(F32)).astype(BF16)
        for g in range(0, N, GROUP):
            total = jnp.dot(
                xp_ref[g + 1 : g + 1 + GROUP].reshape(GROUP * 96, EXT), own_ref[...], preferred_element_type=F32
            )
            left = xp_ref[g : g + GROUP].reshape(GROUP * 96, EXT)
            right = xp_ref[g + 2 : g + 2 + GROUP].reshape(GROUP * 96, EXT)
            side = [
                jnp.dot(left[:, h * PTS : (h + 1) * PTS], left_ref[...], preferred_element_type=F32)
                + jnp.dot(right[:, h * PTS : (h + 1) * PTS], right_ref[...], preferred_element_type=F32)
                for h in range(2)
            ]
            total = total + jnp.concatenate(side, axis=1)
            for i in range(GROUP):
                c = g + i
                y = total[96 * i : 96 * i + 48] + total[96 * i + 48 : 96 * i + 96]
                d = d_ref[c]
                thick = jnp.where(below_top, d - pltpu.roll(d, 44, 0), 0.0) + jnp.where(
                    above_bottom, d - pltpu.roll(d, 4, 0), 0.0
                )
                zero = jnp.zeros((8, EXT), F32)
                load = jnp.concatenate(
                    [a for k in range(3) for a in (zero, lx_ref[c, 8 * k : 8 * k + 8])], axis=0
                )
                stiff = jnp.concatenate([sx_ref[c]] * 6, axis=0)
                v = v_ref[c] + DT * (stiff * y - 0.5 * thick + load)
                v_ref[c] = v
                d_ref[c] = d + DT * v
        return carry

    lax.fori_loop(0, SUBSTEPS, substep, 0)
    for c in range(N):
        if last:
            exponents = []
            for unit in range(6):
                rows = slice(16 * (unit % 3), 16 * (unit % 3) + 16)
                exponents += encode_rows(outs[0], c, unit, (d_ref, v_ref)[unit // 3][c, rows, own])
            outs[0][c, 96:112, :] = to_i16(jnp.concatenate(exponents + exponents[:4], axis=0))
            continue
        for k in range(3):
            rows = slice(16 * k, 16 * k + 16)
            for ref, w in ((d_ref, 0), (v_ref, 1)):
                outs[0][c, w, k] = ref[c, rows, own]
                if not last:
                    halo = slice(48 * w + 16 * k, 48 * w + 16 * k + 16)
                    outs[1][c, halo, :] = ref[c, rows, HALO : 2 * HALO]
                    outs[2][c, halo, :] = ref[c, rows, PTS : PTS + HALO]
        if not last:
            static = st_ref[c]
            v_rows = jnp.concatenate([v_ref[c, 16 * k + 8 : 16 * k + 16, own] for k in range(3)], axis=0)
            speeds = patch_speeds(v_rows, static, node_onehot(static[6:7]))[4:8]
            outs[3][c] = speeds
            outs[4][c] = speeds.astype(BF16)


def solid(last, x, lo, hi, first_lo, first_hi, loading, load_lo, load_hi, static, matrices):


    whole = pl.BlockSpec(memory_space=pltpu.VMEM)

    def full(a):
        return pl.BlockSpec(a.shape, lambda i: (0,) * a.ndim)

    halo = pl.BlockSpec((N, 96, HALO), lambda i: (0, 0, 0))
    stiff = pl.BlockSpec((N, 8, HALO), lambda i: (0, 12, 0))
    outs = [jax.ShapeDtypeStruct((N, 112, PTS), jnp.int16) if last else jax.ShapeDtypeStruct((N, 2, 3, 16, PTS), F32)]
    if not last:
        outs += [jax.ShapeDtypeStruct((N, 96, HALO), F32)] * 2
        outs += [jax.ShapeDtypeStruct((N, QL, PTS), F32), jax.ShapeDtypeStruct((N, QL, PTS), BF16)]
    return pl.pallas_call(
        functools.partial(solid_kernel, last),
        grid=(1,),
        in_specs=[full(x), halo, halo, stiff, stiff]
        + [full(a) for a in (loading, load_lo, load_hi, static, *matrices)],
        out_specs=[full(o) for o in outs],
        out_shape=outs,
        scratch_shapes=[
            pltpu.VMEM((N, 48, EXT), F32),
            pltpu.VMEM((N, 48, EXT), F32),
            pltpu.VMEM((N + 2, 96, EXT), BF16),
            pltpu.VMEM((N, 24, EXT), F32),
            pltpu.VMEM((N, 8, EXT), F32),
        ],
        compiler_params=params(36),
        name="solid_last" if last else "solid",
    )(x, lo, hi, first_lo, first_hi, loading, load_lo, load_hi, static, *matrices)


def exchange(blocks, axis):
    return lax.all_to_all(blocks, axis, split_axis=0, concat_axis=0, tiled=True)


def copies(array, axis):
    return exchange(jnp.broadcast_to(array, (N, *array.shape)), axis)


def from_neighbours(first_rows, last_rows):
    down = [(i, i + 1) for i in range(N - 1)]
    up = [(b, a) for a, b in down]
    return lax.ppermute(last_rows, ROWS, down), lax.ppermute(first_rows, ROWS, up)


def on_device(displacement, velocity, stiffness, wet_position, wet_normal, wet_area, wet_map):
    shape = displacement.shape
    map_row = wet_map.astype(F32)[None]
    static_own = jnp.concatenate([wet_position, wet_normal, map_row, stiffness.reshape(1, PTS)], axis=0)
    source_own = jnp.concatenate([wet_position, wet_normal, wet_area[None], wet_area[None]], axis=0)
    static = copies(static_own, "tcol")
    blocks, speeds_own = pack(
        displacement.reshape(3, PTS, PTS), velocity.reshape(3, PTS, PTS), static_own, source_own
    )
    static, speeds_own = lax.optimization_barrier((static, speeds_own))
    src = copies(speeds_own, ROWS)
    src, blocks = lax.optimization_barrier((src, blocks))
    x = exchange(blocks, "tcol")
    kernel, partial = build(src, static)
    x, partial = lax.optimization_barrier((x, partial))
    speeds, x_first, x_last = first(x, static)
    lo, hi = from_neighbours(x_first, x_last)
    first_lo, first_hi = lo, hi
    matrices = tuple(jnp.asarray(m, BF16) for m in stencil_matrices())
    for repeat in range(COUPLED):
        received = exchange(partial, "tcol")
        loading, load_first, load_last = loads(received, speeds, static)
        load_lo, load_hi = from_neighbours(load_first, load_last)
        last = repeat == COUPLED - 1
        x, *more = solid(last, x, lo, hi, first_lo, first_hi, loading, load_lo, load_hi, static, matrices)
        if last:
            break
        x_first, x_last, speeds, rounded = more
        own = exchange(rounded, "tcol").reshape(LOADS, PTS)
        gathered = copies(own, ROWS)
        partial = product(kernel, gathered)
        partial, x_first = lax.optimization_barrier((partial, x_first))
        lo, hi = from_neighbours(x_first, x_last)
    d, v = unpack(exchange(x, "tcol"))
    return d.reshape(shape), v.reshape(shape)


def solution(mesh):
    state = P(None, ("group", "trow"), "tcol", None)
    points = P(("group", "trow", "tcol"))
    vectors = P(None, ("group", "trow", "tcol"))
    return jax.shard_map(
        on_device,
        mesh=mesh,
        in_specs=(state, state, P(("group", "trow"), "tcol"), vectors, vectors, points, points),
        out_specs=(state, state),
        check_vma=False,
    )
```

```python
import functools
import math

import jax
import jax.numpy as jnp
import numpy as np
from jax import lax
from jax.experimental import pallas as pl
from jax.experimental.pallas import tpu as pltpu
from jax.sharding import PartitionSpec as P

SUBSTEPS = 4
COUPLED = 2
N = 16
PTS = 256
PB = 8
LOADS = 64
SRC = LOADS + 32
QL = 4
HALO = 128
EXT = PTS + 2 * HALO
DT = 0.3
ROWS = ("group", "trow")
F32, BF16 = jnp.float32, jnp.bfloat16


def params(mib):
    return pltpu.CompilerParams(vmem_limit_bytes=mib << 20)


def split3(x):
    hi = x.astype(BF16).astype(F32)
    rest = x - hi
    mid = rest.astype(BF16).astype(F32)
    return hi, mid, (rest - mid).astype(BF16).astype(F32)


def encode(x):
    top = jnp.max(jnp.max(jnp.abs(x), axis=0, keepdims=True), axis=1, keepdims=True)
    exponent = jnp.floor(jnp.log2(jnp.maximum(top, 1e-30))) + 1.0
    scaled = jnp.round(x * jnp.exp2(15.0 - exponent))
    return jnp.clip(scaled, -32767.0, 32767.0), exponent


def to_i16(x):
    return x.astype(jnp.int32).astype(jnp.int16)


def from_i16(x):
    return x.astype(jnp.int32).astype(F32)


def encode_rows(ref, c, unit, x):
    low, e0 = encode(x[:8])
    high, e1 = encode(x[8:])
    ref[c, 16 * unit : 16 * unit + 16, :] = to_i16(jnp.concatenate([low, high], axis=0))
    return [jnp.broadcast_to(e, (1, PTS)) for e in (e0, e1)]


def decode_scales(ref, c):
    return jnp.exp2(from_i16(ref[c, 96:112, :]) - 15.0)


def decode_rows(ref, c, unit, scales):
    x = from_i16(ref[c, 16 * unit : 16 * unit + 16, :])
    return jnp.concatenate(
        [x[8 * h : 8 * h + 8] * scales[2 * unit + h : 2 * unit + h + 1] for h in range(2)], axis=0
    )


def pick_rows(values, onehot):
    rows = values.shape[0]
    parts = jnp.concatenate(split3(values), axis=0).astype(BF16)
    out = jnp.dot(parts, onehot, preferred_element_type=F32)
    return out[:rows] + out[rows : 2 * rows] + out[2 * rows :]


def node_onehot(map_row):
    nodes = lax.broadcasted_iota(jnp.int32, (PTS, PTS), 0).astype(F32)
    return jnp.where(nodes == map_row, 1.0, 0.0).astype(BF16)


STATIC_AT = 112
CODED = 128


def static_scale():
    row = lax.broadcasted_iota(jnp.int32, (8, PTS), 0)
    return jnp.where(row < 6, 4096.0, jnp.where(row == 6, 128.0, 2048.0))


def encode_static(rows):
    scaled = rows * static_scale()
    high = jnp.round(scaled)
    return jnp.concatenate([high, jnp.round((scaled - high) * 32768.0)], axis=0)


def decode_static(block):
    x = from_i16(block)
    scale = static_scale()[:, : block.shape[-1]]
    return (x[:8] + x[8:] * (1.0 / 32768.0)) * (1.0 / scale)


def pack_kernel(d_ref, v_ref, st_ref, so_ref, x_ref, sp_ref):
    exponents = [[] for _ in range(N)]
    speeds = None
    onehot = node_onehot(st_ref[6:7])
    for unit in range(6):
        k = unit % 3
        t = (d_ref, v_ref)[unit // 3][k].T
        for c in range(N):
            rows = [t[l * LOADS + c * QL : l * LOADS + (c + 1) * QL] for l in range(4)]
            exponents[c] += encode_rows(x_ref, c, unit, jnp.concatenate(rows, axis=0))
        if unit >= 3:
            term = pick_rows(t[3 * LOADS :], onehot) * st_ref[3 + k : 4 + k]
            speeds = term if speeds is None else speeds + term
    static = to_i16(encode_static(st_ref[...]))
    for c in range(N):
        x_ref[c, 96:STATIC_AT, :] = to_i16(jnp.concatenate(exponents[c] + exponents[c][:4], axis=0))
        x_ref[c, STATIC_AT:, :] = static
    geometry = list(split3(so_ref[...]))
    sp_ref[...] = jnp.concatenate([speeds] + geometry + geometry[2:], axis=0).astype(BF16)


def pack(d, v, static, source):
    return pl.pallas_call(
        pack_kernel,
        out_shape=[
            jax.ShapeDtypeStruct((N, CODED, PTS), jnp.int16),
            jax.ShapeDtypeStruct((SRC, PTS), BF16),
        ],
        compiler_params=params(16),
        name="pack",
    )(d, v, static, source)


def unpack_kernel(x_ref, d_ref, v_ref, t_ref):
    for c in range(N):
        scales = decode_scales(x_ref, c)
        for unit in range(6):
            rows = decode_rows(x_ref, c, unit, scales)
            for l in range(4):
                at = slice(l * LOADS + c * QL, l * LOADS + (c + 1) * QL)
                t_ref[unit, at, :] = rows[l * QL : (l + 1) * QL]
    for k in range(3):
        d_ref[k] = t_ref[k].T
        v_ref[k] = t_ref[3 + k].T


def unpack(x):
    return pl.pallas_call(
        unpack_kernel,
        out_shape=[jax.ShapeDtypeStruct((3, PTS, PTS), F32)] * 2,
        scratch_shapes=[pltpu.VMEM((6, PTS, PTS), F32)],
        compiler_params=params(16),
        name="unpack",
    )(x)


def feature_rows(parts, order, extra):
    rows = [parts[k][o] for k in range(3) for o in order] + extra
    rows = rows + [jnp.zeros_like(rows[0])] * (32 - len(rows))
    return jnp.concatenate(rows, axis=0)


SOURCE_ORDER = (0, 0, 0, 1, 1, 2)
TARGET_ORDER = (0, 1, 2, 0, 1, 0)
TB = 512


def build_kernel(src_ref, tgt_ref, k_ref, o_ref, fn_ref, fs_ref, sp_ref, mid_ref, e_ref):

    @pl.when(pl.program_id(0) == 0)
    def _():
        total = None
        for j in range(N):
            sp_ref[j * PTS : (j + 1) * PTS, :] = src_ref[j, :LOADS, :].T
            geometry = src_ref[j, LOADS:, :].astype(F32)
            geometry = geometry[:8] + geometry[8:16] + geometry[16:24]
            total = geometry if total is None else total + geometry
        mid_ref[...] = jnp.broadcast_to(jnp.sum(total, axis=1, keepdims=True) * (1.0 / (N * PTS)), (8, PTS))
        for j in range(N):
            geometry = src_ref[j, LOADS:, :].astype(F32)
            geometry = geometry[:8] + geometry[8:16] + geometry[16:24]
            p = [geometry[k : k + 1] - mid_ref[k : k + 1, :] for k in range(3)]
            w = geometry[6:7] * (1.0 / (4.0 * math.pi))
            m = [geometry[3 + k : 4 + k] * w for k in range(3)]
            shift = -(m[0] * p[0] + m[1] * p[1] + m[2] * p[2])
            square = p[0] * p[0] + p[1] * p[1] + p[2] * p[2] + 0.01
            one = jnp.ones_like(shift)
            fn = feature_rows([split3(a) for a in m], SOURCE_ORDER, list(split3(shift)))
            fs = feature_rows([split3(-2.0 * a) for a in p], SOURCE_ORDER, list(split3(square)) + [one] * 3)
            at = slice(j * PTS, (j + 1) * PTS)
            fn_ref[:, at] = fn.astype(BF16)
            fs_ref[:, at] = fs.astype(BF16)

    for b in range(TB // PTS):
        t = [tgt_ref[b, k : k + 1, :] - mid_ref[k : k + 1, :] for k in range(3)]
        square = t[0] * t[0] + t[1] * t[1] + t[2] * t[2]
        one = jnp.ones_like(square)
        g = feature_rows([split3(a) for a in t], TARGET_ORDER, [one] * 3 + list(split3(square))).T.astype(BF16)
        for j in range(N):
            at = slice(j * PTS, (j + 1) * PTS)
            numerator = jnp.dot(g, fn_ref[:, at], preferred_element_type=F32)
            inverse = lax.rsqrt(jnp.dot(g, fs_ref[:, at], preferred_element_type=F32))
            k_ref[b * PTS : (b + 1) * PTS, at] = (numerator * inverse * (inverse * inverse)).astype(BF16)
    total = jnp.dot(k_ref[...], sp_ref[...], preferred_element_type=F32).T
    write_partial(total, o_ref, e_ref)


def write_partial(total, o_ref, e_ref):
    step = pl.program_id(0)
    width = total.shape[1]
    lane = lax.broadcasted_iota(jnp.int32, (LOADS, 128), 1)
    for b in range(width // TB):
        part = total[:, b * TB : (b + 1) * TB]
        top = jnp.max(jnp.abs(part), axis=1, keepdims=True)
        exponent = jnp.floor(jnp.log2(jnp.maximum(top, 1e-30))) + 1.0
        part = to_i16(jnp.clip(jnp.round(part * jnp.exp2(15.0 - exponent)), -32767.0, 32767.0))
        at = pl.ds(pl.multiple_of(step * width + b * TB, TB), TB)
        for c in range(N):
            o_ref[c, :, at] = part[c * QL : (c + 1) * QL]
        index = step * (width // TB) + b
        e_ref[...] = jnp.where(lane == index, exponent, jnp.where(index == 0, 0.0, e_ref[...]))

    @pl.when(step == pl.num_programs(0) - 1)
    def _():
        exponents = to_i16(e_ref[...])
        for c in range(N):
            o_ref[c, :, N * PTS :] = exponents[c * QL : (c + 1) * QL]


def build(src, tgt):
    points = N * PTS
    return pl.pallas_call(
        build_kernel,
        grid=(points // TB,),
        in_specs=[
            pl.BlockSpec((N, SRC, PTS), lambda i: (0, 0, 0)),
            pl.BlockSpec((TB // PTS, 8, PTS), lambda i: (i, 0, 0)),
        ],
        out_specs=[
            pl.BlockSpec((TB, points), lambda i: (i, 0)),
            pl.BlockSpec((N, QL, points + 128), lambda i: (0, 0, 0)),
        ],
        out_shape=[
            jax.ShapeDtypeStruct((points, points), BF16),
            jax.ShapeDtypeStruct((N, QL, points + 128), jnp.int16),
        ],
        scratch_shapes=[
            pltpu.VMEM((32, points), BF16),
            pltpu.VMEM((32, points), BF16),
            pltpu.VMEM((points, LOADS), BF16),
            pltpu.VMEM((8, PTS), F32),
            pltpu.VMEM((LOADS, 128), F32),
        ],
        compiler_params=params(24),
        cost_estimate=pl.CostEstimate(flops=20 << 30, bytes_accessed=100 << 20, transcendentals=16 << 20),
        name="build",
    )(src, tgt)


TB2 = 1024


def product_kernel(k_ref, own_ref, o_ref, sp_ref, e_ref):
    @pl.when(pl.program_id(0) == 0)
    def _():
        for j in range(N):
            sp_ref[j * PTS : (j + 1) * PTS, :] = own_ref[j].T

    total = jnp.dot(k_ref[...], sp_ref[...], preferred_element_type=F32).T
    write_partial(total, o_ref, e_ref)


def product(kernel, sp):
    points = N * PTS
    return pl.pallas_call(
        product_kernel,
        grid=(points // TB2,),
        in_specs=[
            pl.BlockSpec((TB2, points), lambda i: (i, 0)),
            pl.BlockSpec((N, LOADS, PTS), lambda i: (0, 0, 0)),
        ],
        out_specs=pl.BlockSpec((N, QL, points + 128), lambda i: (0, 0, 0)),
        out_shape=jax.ShapeDtypeStruct((N, QL, points + 128), jnp.int16),
        scratch_shapes=[pltpu.VMEM((points, LOADS), BF16), pltpu.VMEM((LOADS, 128), F32)],
        compiler_params=params(24),
        cost_estimate=pl.CostEstimate(flops=4 << 30, bytes_accessed=40 << 20, transcendentals=0),
        name="product",
    )(kernel, sp)


def patch_speeds(v_rows, static, onehot):
    picked = pick_rows(v_rows, onehot)
    return sum(static[3 + k : 4 + k] * picked[8 * k : 8 * k + 8] for k in range(3))


def first_kernel(x_ref, st_ref, s_ref):
    for c in range(N):
        static = st_ref[c]
        scales = decode_scales(x_ref, c)
        v_rows = jnp.concatenate([decode_rows(x_ref, c, 3 + k, scales)[8:] for k in range(3)], axis=0)
        s_ref[c] = patch_speeds(v_rows, static, node_onehot(static[6:7]))[4:8]


def first(x, static):
    return pl.pallas_call(
        first_kernel,
        out_shape=jax.ShapeDtypeStruct((N, QL, PTS), F32),
        compiler_params=params(20),
        name="first",
    )(x, static)


def load_kernel(rec_ref, s_ref, st_ref, l_ref, first_ref, last_ref):
    scales = [jnp.exp2(from_i16(rec_ref[j, :, N * PTS :]) - 15.0) for j in range(N)]
    for c in range(N):
        at = slice(c * PTS, (c + 1) * PTS)
        index = c * PTS // TB
        pressure = 0.5 * s_ref[c]
        for j in range(N):
            pressure = pressure + from_i16(rec_ref[j, :, at]) * scales[j][:, index : index + 1]
        pressure = jnp.concatenate([jnp.zeros_like(pressure), pressure], axis=0)
        static = st_ref[c]
        parts = jnp.concatenate([-(static[3 + k : 4 + k] * pressure) for k in range(3)], axis=0)
        parts = jnp.concatenate(split3(parts), axis=0).astype(BF16)
        out = lax.dot_general(
            parts, node_onehot(static[6:7]), (((1,), (1,)), ((), ())), preferred_element_type=F32
        )
        loading = out[:24] + out[24:48] + out[48:]
        l_ref[c] = loading
        for k in range(3):
            first_ref[c, k] = loading[8 * k + 4 : 8 * k + 8, :HALO]
            last_ref[c, k] = loading[8 * k + 4 : 8 * k + 8, PTS - HALO :]


def loads(rec, speeds, static):
    return pl.pallas_call(
        load_kernel,
        out_shape=[
            jax.ShapeDtypeStruct((N, 24, PTS), F32),
            jax.ShapeDtypeStruct((N, 3, QL, HALO), F32),
            jax.ShapeDtypeStruct((N, 3, QL, HALO), F32),
        ],
        compiler_params=params(20),
        name="loads",
    )(rec, speeds, static)


def stencil_matrices():
    taps = {0: -16.0, 1: 1.0, 2: 1.0, 3: 2.0}
    count = EXT // PB
    own = np.zeros((count, PB, count, PB), np.float32)
    left = np.zeros((PTS // PB, PB, PTS // PB, PB), np.float32)
    right = np.zeros_like(left)
    for a in range(count):
        for b in range(PB):
            own[a, b, a, b] = taps[0]
            for o in (1, 2, 3):
                for s in (o, -o):
                    if 0 <= a + s < count:
                        own[a + s, b, a, b] = taps[o]
                    if 0 <= b + s < PB:
                        own[a, b + s, a, b] = taps[o]
                    elif a < PTS // PB:
                        (left if s < 0 else right)[a, (b + s) % PB, a, b] = taps[o]
    return own.reshape(EXT, EXT), left.reshape(PTS, PTS), right.reshape(PTS, PTS)


GROUP = 4


def halo_stiffness(ref, c):
    return jnp.broadcast_to(decode_static(ref[c])[7:8] * (1.0 / 12.0), (8, HALO))


def solid_kernel(last, *refs):
    if last:
        x_ref, lo_ref, hi_ref, *refs = refs
    else:
        x_ref, lo_ref, hi_ref = coded = refs[:3]
        refs = refs[3:]
    slo_ref, shi_ref, l_ref, llo_ref, lhi_ref, st_ref, own_ref, left_ref, right_ref, *outs = refs
    *outs, d_ref, v_ref, xp_ref, lx_ref, sx_ref = outs
    own = slice(HALO, HALO + PTS)
    xp_ref[0] = jnp.zeros_like(xp_ref[0])
    xp_ref[N + 1] = jnp.zeros_like(xp_ref[0])
    for c in range(N):
        if not last:
            for source, at in zip(coded, (own, slice(0, HALO), slice(HALO + PTS, EXT))):
                scales = decode_scales(source, c)
                for unit in range(6):
                    rows = slice(16 * (unit % 3), 16 * (unit % 3) + 16)
                    (d_ref, v_ref)[unit // 3][c, rows, at] = decode_rows(source, c, unit, scales)
        for k in range(3):
            rows = slice(16 * k, 16 * k + 16)
            for ref, w in ((d_ref, 0), (v_ref, 1)) if last else ():
                halo = slice(48 * w + 16 * k, 48 * w + 16 * k + 16)
                ref[c, rows, :HALO] = lo_ref[c, halo, :]
                ref[c, rows, own] = x_ref[c, w, k]
                ref[c, rows, HALO + PTS :] = hi_ref[c, halo, :]
            zero = jnp.zeros((4, HALO), F32)
            lx_ref[c, 8 * k : 8 * k + 8, :HALO] = jnp.concatenate([zero, llo_ref[c, k]], axis=0)
            lx_ref[c, 8 * k : 8 * k + 8, own] = l_ref[c, 8 * k : 8 * k + 8]
            lx_ref[c, 8 * k : 8 * k + 8, HALO + PTS :] = jnp.concatenate([zero, lhi_ref[c, k]], axis=0)
        sx_ref[c, :, :HALO] = halo_stiffness(slo_ref, c)
        sx_ref[c, :, own] = jnp.broadcast_to(st_ref[c, 7:8, :], (8, PTS)) * (1.0 / 12.0)
        sx_ref[c, :, HALO + PTS :] = halo_stiffness(shi_ref, c)
    layer = lax.rem(lax.broadcasted_iota(jnp.int32, (48, EXT), 0), 16)
    below_top, above_bottom = layer < 12, layer >= 4

    def substep(_, carry):
        for c in range(N):
            d = d_ref[c]
            hi = d.astype(BF16)
            xp_ref[c + 1, :48] = hi
            xp_ref[c + 1, 48:] = (d - hi.astype(F32)).astype(BF16)
        for g in range(0, N, GROUP):
            total = jnp.dot(
                xp_ref[g + 1 : g + 1 + GROUP].reshape(GROUP * 96, EXT), own_ref[...], preferred_element_type=F32
            )
            left = xp_ref[g : g + GROUP].reshape(GROUP * 96, EXT)
            right = xp_ref[g + 2 : g + 2 + GROUP].reshape(GROUP * 96, EXT)
            side = [
                jnp.dot(left[:, h * PTS : (h + 1) * PTS], left_ref[...], preferred_element_type=F32)
                + jnp.dot(right[:, h * PTS : (h + 1) * PTS], right_ref[...], preferred_element_type=F32)
                for h in range(2)
            ]
            total = total + jnp.concatenate(side, axis=1)
            for i in range(GROUP):
                c = g + i
                y = total[96 * i : 96 * i + 48] + total[96 * i + 48 : 96 * i + 96]
                d = d_ref[c]
                thick = jnp.where(below_top, d - pltpu.roll(d, 44, 0), 0.0) + jnp.where(
                    above_bottom, d - pltpu.roll(d, 4, 0), 0.0
                )
                zero = jnp.zeros((8, EXT), F32)
                load = jnp.concatenate(
                    [a for k in range(3) for a in (zero, lx_ref[c, 8 * k : 8 * k + 8])], axis=0
                )
                stiff = jnp.concatenate([sx_ref[c]] * 6, axis=0)
                v = v_ref[c] + DT * (stiff * y - 0.5 * thick + load)
                v_ref[c] = v
                d_ref[c] = d + DT * v
        return carry

    lax.fori_loop(0, SUBSTEPS, substep, 0)
    for c in range(N):
        if last:
            exponents = []
            for unit in range(6):
                rows = slice(16 * (unit % 3), 16 * (unit % 3) + 16)
                exponents += encode_rows(outs[0], c, unit, (d_ref, v_ref)[unit // 3][c, rows, own])
            outs[0][c, 96:112, :] = to_i16(jnp.concatenate(exponents + exponents[:4], axis=0))
            continue
        for k in range(3):
            rows = slice(16 * k, 16 * k + 16)
            for ref, w in ((d_ref, 0), (v_ref, 1)):
                outs[0][c, w, k] = ref[c, rows, own]
                if not last:
                    halo = slice(48 * w + 16 * k, 48 * w + 16 * k + 16)
                    outs[1][c, halo, :] = ref[c, rows, HALO : 2 * HALO]
                    outs[2][c, halo, :] = ref[c, rows, PTS : PTS + HALO]
        if not last:
            static = st_ref[c]
            v_rows = jnp.concatenate([v_ref[c, 16 * k + 8 : 16 * k + 16, own] for k in range(3)], axis=0)
            speeds = patch_speeds(v_rows, static, node_onehot(static[6:7]))[4:8]
            outs[3][c] = speeds
            outs[4][c] = speeds.astype(BF16)


def solid(last, x, lo, hi, first_lo, first_hi, loading, load_lo, load_hi, static, matrices):


    whole = pl.BlockSpec(memory_space=pltpu.VMEM)

    def full(a):
        return pl.BlockSpec(a.shape, lambda i: (0,) * a.ndim)

    halo = full(lo)
    stiff = pl.BlockSpec((N, 16, HALO), lambda i: (0, STATIC_AT // 16, 0))
    outs = [jax.ShapeDtypeStruct((N, STATIC_AT, PTS), jnp.int16) if last else jax.ShapeDtypeStruct((N, 2, 3, 16, PTS), F32)]
    if not last:
        outs += [jax.ShapeDtypeStruct((N, 96, HALO), F32)] * 2
        outs += [jax.ShapeDtypeStruct((N, QL, PTS), F32), jax.ShapeDtypeStruct((N, QL, PTS), BF16)]
    return pl.pallas_call(
        functools.partial(solid_kernel, last),
        grid=(1,),
        in_specs=[full(x), halo, halo, stiff, stiff]
        + [full(a) for a in (loading, load_lo, load_hi, static, *matrices)],
        out_specs=[full(o) for o in outs],
        out_shape=outs,
        scratch_shapes=[
            pltpu.VMEM((N, 48, EXT), F32),
            pltpu.VMEM((N, 48, EXT), F32),
            pltpu.VMEM((N + 2, 96, EXT), BF16),
            pltpu.VMEM((N, 24, EXT), F32),
            pltpu.VMEM((N, 8, EXT), F32),
        ],
        compiler_params=params(36),
        name="solid_last" if last else "solid",
    )(x, lo, hi, first_lo, first_hi, loading, load_lo, load_hi, static, *matrices)


def exchange(blocks, axis):
    return lax.all_to_all(blocks, axis, split_axis=0, concat_axis=0, tiled=True)


def copies(array, axis):
    return exchange(jnp.broadcast_to(array, (N, *array.shape)), axis)


def from_neighbours(first_rows, last_rows):
    down = [(i, i + 1) for i in range(N - 1)]
    up = [(b, a) for a, b in down]
    return lax.ppermute(last_rows, ROWS, down), lax.ppermute(first_rows, ROWS, up)


def on_device(displacement, velocity, stiffness, wet_position, wet_normal, wet_area, wet_map):
    shape = displacement.shape
    map_row = wet_map.astype(F32)[None]
    static_own = jnp.concatenate([wet_position, wet_normal, map_row, stiffness.reshape(1, PTS)], axis=0)
    source_own = jnp.concatenate([wet_position, wet_normal, wet_area[None], wet_area[None]], axis=0)
    static = copies(static_own, "tcol")
    coded, source = pack(
        displacement.reshape(3, PTS, PTS), velocity.reshape(3, PTS, PTS), static_own, source_own
    )
    static, source = lax.optimization_barrier((static, source))
    src = copies(source, ROWS)
    src, coded = lax.optimization_barrier((src, coded))
    x = exchange(coded, "tcol")
    kernel, partial = build(src, static)
    x, partial = lax.optimization_barrier((x, partial))
    x_first, x_last = x[:, :, :HALO], x[:, :, PTS - HALO :]
    lo, hi = from_neighbours(x_first, x_last)
    first_lo, first_hi = lo, hi
    speeds = first(x, static)
    matrices = tuple(jnp.asarray(m, BF16) for m in stencil_matrices())
    for repeat in range(COUPLED):
        received = exchange(partial, "tcol")
        loading, load_first, load_last = loads(received, speeds, static)
        load_lo, load_hi = from_neighbours(load_first, load_last)
        last = repeat == COUPLED - 1
        x, *more = solid(last, x, lo, hi, first_lo, first_hi, loading, load_lo, load_hi, static, matrices)
        if last:
            break
        x_first, x_last, speeds, rounded = more
        own = exchange(rounded, "tcol").reshape(LOADS, PTS)
        gathered = copies(own, ROWS)
        partial = product(kernel, gathered)
        partial, x_first = lax.optimization_barrier((partial, x_first))
        lo, hi = from_neighbours(x_first, x_last)
    d, v = unpack(exchange(x, "tcol"))
    return d.reshape(shape), v.reshape(shape)


def solution(mesh):
    state = P(None, ("group", "trow"), "tcol", None)
    points = P(("group", "trow", "tcol"))
    vectors = P(None, ("group", "trow", "tcol"))
    return jax.shard_map(
        on_device,
        mesh=mesh,
        in_specs=(state, state, P(("group", "trow"), "tcol"), vectors, vectors, points, points),
        out_specs=(state, state),
        check_vma=False,
    )
```

```python
import functools
import math

import jax
import jax.numpy as jnp
import numpy as np
from jax import lax
from jax.experimental import pallas as pl
from jax.experimental.pallas import tpu as pltpu
from jax.sharding import PartitionSpec as P

SUBSTEPS = 4
COUPLED = 2
N = 16
PTS = 256
PB = 8
LOADS = 64
SRC = LOADS + 32
QL = 4
HALO = 128
EXT = PTS + 2 * HALO
DT = 0.3
ROWS = ("group", "trow")
F32, BF16 = jnp.float32, jnp.bfloat16


def params(mib):
    return pltpu.CompilerParams(vmem_limit_bytes=mib << 20)


def split3(x):
    hi = x.astype(BF16).astype(F32)
    rest = x - hi
    mid = rest.astype(BF16).astype(F32)
    return hi, mid, (rest - mid).astype(BF16).astype(F32)


def encode(x):
    top = jnp.max(jnp.max(jnp.abs(x), axis=0, keepdims=True), axis=1, keepdims=True)
    exponent = jnp.floor(jnp.log2(jnp.maximum(top, 1e-30))) + 1.0
    scaled = jnp.round(x * jnp.exp2(15.0 - exponent))
    return jnp.clip(scaled, -32767.0, 32767.0), exponent


def to_i16(x):
    return x.astype(jnp.int32).astype(jnp.int16)


def from_i16(x):
    return x.astype(jnp.int32).astype(F32)


def encode_rows(ref, c, unit, x):
    values, exponent = encode(x)
    ref[c, 16 * unit : 16 * unit + 16, :] = to_i16(values)
    return jnp.broadcast_to(exponent, (1, PTS))


def write_exponents(ref, c, rows):
    ref[c, 96:104, :] = to_i16(jnp.concatenate(rows + rows[:2], axis=0))


def decode_scales(ref, c):
    return jnp.exp2(from_i16(ref[c, 96:104, :]) - 15.0)


def decode_rows(ref, c, unit, scales):
    return from_i16(ref[c, 16 * unit : 16 * unit + 16, :]) * scales[unit : unit + 1]


def pick_rows(values, onehot):
    rows = values.shape[0]
    parts = jnp.concatenate(split3(values), axis=0).astype(BF16)
    out = jnp.dot(parts, onehot, preferred_element_type=F32)
    return out[:rows] + out[rows : 2 * rows] + out[2 * rows :]


def node_onehot(map_row):
    nodes = lax.broadcasted_iota(jnp.int32, (PTS, PTS), 0).astype(F32)
    return jnp.where(nodes == map_row, 1.0, 0.0).astype(BF16)


FINAL = 104
STATIC_AT = 112
CODED = 128


def static_scale():
    row = lax.broadcasted_iota(jnp.int32, (8, PTS), 0)
    return jnp.where(row < 6, 4096.0, jnp.where(row == 6, 128.0, 2048.0))


def encode_static(rows):
    scaled = rows * static_scale()
    high = jnp.round(scaled)
    return jnp.concatenate([high, jnp.round((scaled - high) * 32768.0)], axis=0)


def decode_static(block):
    x = from_i16(block)
    scale = static_scale()[:, : block.shape[-1]]
    return (x[:8] + x[8:] * (1.0 / 32768.0)) * (1.0 / scale)


def pack_kernel(d_ref, v_ref, st_ref, so_ref, x_ref, sp_ref):
    exponents = [[] for _ in range(N)]
    speeds = None
    onehot = node_onehot(st_ref[6:7])
    for unit in range(6):
        k = unit % 3
        t = (d_ref, v_ref)[unit // 3][k].T
        for c in range(N):
            rows = [t[l * LOADS + c * QL : l * LOADS + (c + 1) * QL] for l in range(4)]
            exponents[c].append(encode_rows(x_ref, c, unit, jnp.concatenate(rows, axis=0)))
        if unit >= 3:
            term = pick_rows(t[3 * LOADS :], onehot) * st_ref[3 + k : 4 + k]
            speeds = term if speeds is None else speeds + term
    static = to_i16(encode_static(st_ref[...]))
    for c in range(N):
        write_exponents(x_ref, c, exponents[c])
        x_ref[c, 104:STATIC_AT, :] = jnp.zeros((8, PTS), jnp.int16)
        x_ref[c, STATIC_AT:, :] = static
    geometry = list(split3(so_ref[...]))
    sp_ref[...] = jnp.concatenate([speeds] + geometry + geometry[2:], axis=0).astype(BF16)


def pack(d, v, static, source):
    return pl.pallas_call(
        pack_kernel,
        out_shape=[
            jax.ShapeDtypeStruct((N, CODED, PTS), jnp.int16),
            jax.ShapeDtypeStruct((SRC, PTS), BF16),
        ],
        compiler_params=params(16),
        name="pack",
    )(d, v, static, source)


def unpack_kernel(x_ref, d_ref, v_ref, t_ref):
    for c in range(N):
        scales = decode_scales(x_ref, c)
        for unit in range(6):
            rows = decode_rows(x_ref, c, unit, scales)
            for l in range(4):
                at = slice(l * LOADS + c * QL, l * LOADS + (c + 1) * QL)
                t_ref[unit, at, :] = rows[l * QL : (l + 1) * QL]
    for k in range(3):
        d_ref[k] = t_ref[k].T
        v_ref[k] = t_ref[3 + k].T


def unpack(x):
    return pl.pallas_call(
        unpack_kernel,
        out_shape=[jax.ShapeDtypeStruct((3, PTS, PTS), F32)] * 2,
        scratch_shapes=[pltpu.VMEM((6, PTS, PTS), F32)],
        compiler_params=params(16),
        name="unpack",
    )(x)


def feature_rows(parts, order, extra):
    rows = [parts[k][o] for k in range(3) for o in order] + extra
    rows = rows + [jnp.zeros_like(rows[0])] * (32 - len(rows))
    return jnp.concatenate(rows, axis=0)


SOURCE_ORDER = (0, 0, 0, 1, 1, 2)
TARGET_ORDER = (0, 1, 2, 0, 1, 0)
TB = 512


def build_kernel(src_ref, tgt_ref, k_ref, o_ref, fn_ref, fs_ref, sp_ref, mid_ref, e_ref):

    @pl.when(pl.program_id(0) == 0)
    def _():
        total = None
        for j in range(N):
            sp_ref[j * PTS : (j + 1) * PTS, :] = src_ref[j, :LOADS, :].T
            geometry = src_ref[j, LOADS:, :].astype(F32)
            geometry = geometry[:8] + geometry[8:16] + geometry[16:24]
            total = geometry if total is None else total + geometry
        mid_ref[...] = jnp.broadcast_to(jnp.sum(total, axis=1, keepdims=True) * (1.0 / (N * PTS)), (8, PTS))
        for j in range(N):
            geometry = src_ref[j, LOADS:, :].astype(F32)
            geometry = geometry[:8] + geometry[8:16] + geometry[16:24]
            p = [geometry[k : k + 1] - mid_ref[k : k + 1, :] for k in range(3)]
            w = geometry[6:7] * (1.0 / (4.0 * math.pi))
            m = [geometry[3 + k : 4 + k] * w for k in range(3)]
            shift = -(m[0] * p[0] + m[1] * p[1] + m[2] * p[2])
            square = p[0] * p[0] + p[1] * p[1] + p[2] * p[2] + 0.01
            one = jnp.ones_like(shift)
            fn = feature_rows([split3(a) for a in m], SOURCE_ORDER, list(split3(shift)))
            fs = feature_rows([split3(-2.0 * a) for a in p], SOURCE_ORDER, list(split3(square)) + [one] * 3)
            at = slice(j * PTS, (j + 1) * PTS)
            fn_ref[:, at] = fn.astype(BF16)
            fs_ref[:, at] = fs.astype(BF16)

    for b in range(TB // PTS):
        t = [tgt_ref[b, k : k + 1, :] - mid_ref[k : k + 1, :] for k in range(3)]
        square = t[0] * t[0] + t[1] * t[1] + t[2] * t[2]
        one = jnp.ones_like(square)
        g = feature_rows([split3(a) for a in t], TARGET_ORDER, [one] * 3 + list(split3(square))).T.astype(BF16)
        for j in range(N):
            at = slice(j * PTS, (j + 1) * PTS)
            numerator = jnp.dot(g, fn_ref[:, at], preferred_element_type=F32)
            inverse = lax.rsqrt(jnp.dot(g, fs_ref[:, at], preferred_element_type=F32))
            k_ref[b * PTS : (b + 1) * PTS, at] = (numerator * inverse * (inverse * inverse)).astype(BF16)
    total = jnp.dot(k_ref[...], sp_ref[...], preferred_element_type=F32).T
    write_partial(total, o_ref, e_ref)


def write_partial(total, o_ref, e_ref):
    step = pl.program_id(0)
    width = total.shape[1]
    lane = lax.broadcasted_iota(jnp.int32, (LOADS, 128), 1)
    for b in range(width // TB):
        part = total[:, b * TB : (b + 1) * TB]
        top = jnp.max(jnp.abs(part), axis=1, keepdims=True)
        exponent = jnp.floor(jnp.log2(jnp.maximum(top, 1e-30))) + 1.0
        part = to_i16(jnp.clip(jnp.round(part * jnp.exp2(15.0 - exponent)), -32767.0, 32767.0))
        at = pl.ds(pl.multiple_of(step * width + b * TB, TB), TB)
        for c in range(N):
            o_ref[c, :, at] = part[c * QL : (c + 1) * QL]
        index = step * (width // TB) + b
        e_ref[...] = jnp.where(lane == index, exponent, jnp.where(index == 0, 0.0, e_ref[...]))

    @pl.when(step == pl.num_programs(0) - 1)
    def _():
        exponents = to_i16(e_ref[...])
        for c in range(N):
            o_ref[c, :, N * PTS :] = exponents[c * QL : (c + 1) * QL]


def build(src, tgt):
    points = N * PTS
    return pl.pallas_call(
        build_kernel,
        grid=(points // TB,),
        in_specs=[
            pl.BlockSpec((N, SRC, PTS), lambda i: (0, 0, 0)),
            pl.BlockSpec((TB // PTS, 8, PTS), lambda i: (i, 0, 0)),
        ],
        out_specs=[
            pl.BlockSpec((TB, points), lambda i: (i, 0)),
            pl.BlockSpec((N, QL, points + 128), lambda i: (0, 0, 0)),
        ],
        out_shape=[
            jax.ShapeDtypeStruct((points, points), BF16),
            jax.ShapeDtypeStruct((N, QL, points + 128), jnp.int16),
        ],
        scratch_shapes=[
            pltpu.VMEM((32, points), BF16),
            pltpu.VMEM((32, points), BF16),
            pltpu.VMEM((points, LOADS), BF16),
            pltpu.VMEM((8, PTS), F32),
            pltpu.VMEM((LOADS, 128), F32),
        ],
        compiler_params=params(24),
        cost_estimate=pl.CostEstimate(flops=20 << 30, bytes_accessed=100 << 20, transcendentals=16 << 20),
        name="build",
    )(src, tgt)


TB2 = 1024


def product_kernel(k_ref, own_ref, o_ref, sp_ref, e_ref):
    @pl.when(pl.program_id(0) == 0)
    def _():
        for j in range(N):
            sp_ref[j * PTS : (j + 1) * PTS, :] = own_ref[j].T

    total = jnp.dot(k_ref[...], sp_ref[...], preferred_element_type=F32).T
    write_partial(total, o_ref, e_ref)


def product(kernel, sp):
    points = N * PTS
    return pl.pallas_call(
        product_kernel,
        grid=(points // TB2,),
        in_specs=[
            pl.BlockSpec((TB2, points), lambda i: (i, 0)),
            pl.BlockSpec((N, LOADS, PTS), lambda i: (0, 0, 0)),
        ],
        out_specs=pl.BlockSpec((N, QL, points + 128), lambda i: (0, 0, 0)),
        out_shape=jax.ShapeDtypeStruct((N, QL, points + 128), jnp.int16),
        scratch_shapes=[pltpu.VMEM((points, LOADS), BF16), pltpu.VMEM((LOADS, 128), F32)],
        compiler_params=params(24),
        cost_estimate=pl.CostEstimate(flops=4 << 30, bytes_accessed=40 << 20, transcendentals=0),
        name="product",
    )(kernel, sp)


def patch_speeds(v_rows, static, onehot):
    picked = pick_rows(v_rows, onehot)
    return sum(static[3 + k : 4 + k] * picked[8 * k : 8 * k + 8] for k in range(3))


def first_kernel(x_ref, st_ref, s_ref):
    for c in range(N):
        static = st_ref[c]
        scales = decode_scales(x_ref, c)
        v_rows = jnp.concatenate([decode_rows(x_ref, c, 3 + k, scales)[8:] for k in range(3)], axis=0)
        s_ref[c] = patch_speeds(v_rows, static, node_onehot(static[6:7]))[4:8]


def first(x, static):
    return pl.pallas_call(
        first_kernel,
        out_shape=jax.ShapeDtypeStruct((N, QL, PTS), F32),
        compiler_params=params(20),
        name="first",
    )(x, static)


def load_kernel(rec_ref, s_ref, st_ref, l_ref, first_ref, last_ref):
    scales = [jnp.exp2(from_i16(rec_ref[j, :, N * PTS :]) - 15.0) for j in range(N)]
    for c in range(N):
        at = slice(c * PTS, (c + 1) * PTS)
        index = c * PTS // TB
        pressure = 0.5 * s_ref[c]
        for j in range(N):
            pressure = pressure + from_i16(rec_ref[j, :, at]) * scales[j][:, index : index + 1]
        pressure = jnp.concatenate([jnp.zeros_like(pressure), pressure], axis=0)
        static = st_ref[c]
        parts = jnp.concatenate([-(static[3 + k : 4 + k] * pressure) for k in range(3)], axis=0)
        parts = jnp.concatenate(split3(parts), axis=0).astype(BF16)
        out = lax.dot_general(
            parts, node_onehot(static[6:7]), (((1,), (1,)), ((), ())), preferred_element_type=F32
        )
        loading = out[:24] + out[24:48] + out[48:]
        l_ref[c] = loading
        for k in range(3):
            first_ref[c, k] = loading[8 * k + 4 : 8 * k + 8, :HALO]
            last_ref[c, k] = loading[8 * k + 4 : 8 * k + 8, PTS - HALO :]


def loads(rec, speeds, static):
    return pl.pallas_call(
        load_kernel,
        out_shape=[
            jax.ShapeDtypeStruct((N, 24, PTS), F32),
            jax.ShapeDtypeStruct((N, 3, QL, HALO), F32),
            jax.ShapeDtypeStruct((N, 3, QL, HALO), F32),
        ],
        compiler_params=params(20),
        name="loads",
    )(rec, speeds, static)


def stencil_matrices():
    taps = {0: -16.0, 1: 1.0, 2: 1.0, 3: 2.0}
    count = EXT // PB
    own = np.zeros((count, PB, count, PB), np.float32)
    left = np.zeros((PTS // PB, PB, PTS // PB, PB), np.float32)
    right = np.zeros_like(left)
    for a in range(count):
        for b in range(PB):
            own[a, b, a, b] = taps[0]
            for o in (1, 2, 3):
                for s in (o, -o):
                    if 0 <= a + s < count:
                        own[a + s, b, a, b] = taps[o]
                    if 0 <= b + s < PB:
                        own[a, b + s, a, b] = taps[o]
                    elif a < PTS // PB:
                        (left if s < 0 else right)[a, (b + s) % PB, a, b] = taps[o]
    return own.reshape(EXT, EXT), left.reshape(PTS, PTS), right.reshape(PTS, PTS)


GROUP = 4


def halo_stiffness(ref, c):
    return jnp.broadcast_to(decode_static(ref[c])[7:8] * (1.0 / 12.0), (8, HALO))


def solid_kernel(last, *refs):
    if last:
        x_ref, lo_ref, hi_ref, *refs = refs
    else:
        x_ref, lo_ref, hi_ref = coded = refs[:3]
        refs = refs[3:]
    slo_ref, shi_ref, l_ref, llo_ref, lhi_ref, st_ref, own_ref, left_ref, right_ref, *outs = refs
    *outs, d_ref, v_ref, xp_ref, lx_ref, sx_ref = outs
    own = slice(HALO, HALO + PTS)
    xp_ref[0] = jnp.zeros_like(xp_ref[0])
    xp_ref[N + 1] = jnp.zeros_like(xp_ref[0])
    for c in range(N):
        if not last:
            for source, at in zip(coded, (own, slice(0, HALO), slice(HALO + PTS, EXT))):
                scales = decode_scales(source, c)
                for unit in range(6):
                    rows = slice(16 * (unit % 3), 16 * (unit % 3) + 16)
                    (d_ref, v_ref)[unit // 3][c, rows, at] = decode_rows(source, c, unit, scales)
        for k in range(3):
            rows = slice(16 * k, 16 * k + 16)
            for ref, w in ((d_ref, 0), (v_ref, 1)) if last else ():
                halo = slice(48 * w + 16 * k, 48 * w + 16 * k + 16)
                ref[c, rows, :HALO] = lo_ref[c, halo, :]
                ref[c, rows, own] = x_ref[c, w, k]
                ref[c, rows, HALO + PTS :] = hi_ref[c, halo, :]
            zero = jnp.zeros((4, HALO), F32)
            lx_ref[c, 8 * k : 8 * k + 8, :HALO] = jnp.concatenate([zero, llo_ref[c, k]], axis=0)
            lx_ref[c, 8 * k : 8 * k + 8, own] = l_ref[c, 8 * k : 8 * k + 8]
            lx_ref[c, 8 * k : 8 * k + 8, HALO + PTS :] = jnp.concatenate([zero, lhi_ref[c, k]], axis=0)
        sx_ref[c, :, :HALO] = halo_stiffness(slo_ref, c)
        sx_ref[c, :, own] = jnp.broadcast_to(st_ref[c, 7:8, :], (8, PTS)) * (1.0 / 12.0)
        sx_ref[c, :, HALO + PTS :] = halo_stiffness(shi_ref, c)
    layer = lax.rem(lax.broadcasted_iota(jnp.int32, (48, EXT), 0), 16)
    below_top, above_bottom = layer < 12, layer >= 4

    def split():
        for c in range(N):
            d = d_ref[c]
            hi = d.astype(BF16)
            xp_ref[c + 1, :48] = hi
            xp_ref[c + 1, 48:] = (d - hi.astype(F32)).astype(BF16)

    def update(lanes, halves):
        count = lanes.stop - lanes.start
        for g in range(0, N, GROUP):
            total = jnp.dot(
                xp_ref[g + 1 : g + 1 + GROUP].reshape(GROUP * 96, EXT),
                own_ref[:, lanes],
                preferred_element_type=F32,
            )
            left = xp_ref[g : g + GROUP].reshape(GROUP * 96, EXT)
            right = xp_ref[g + 2 : g + 2 + GROUP].reshape(GROUP * 96, EXT)
            side = [
                jnp.dot(left[:, at], left_ref[...], preferred_element_type=F32)
                + jnp.dot(right[:, at], right_ref[...], preferred_element_type=F32)
                for at in halves
            ]
            total = total + jnp.concatenate(side, axis=1)
            for i in range(GROUP):
                c = g + i
                y = total[96 * i : 96 * i + 48] + total[96 * i + 48 : 96 * i + 96]
                d = d_ref[c, :, lanes]
                thick = jnp.where(below_top[:, :count], d - pltpu.roll(d, 44, 0), 0.0) + jnp.where(
                    above_bottom[:, :count], d - pltpu.roll(d, 4, 0), 0.0
                )
                zero = jnp.zeros((8, count), F32)
                load = jnp.concatenate(
                    [a for k in range(3) for a in (zero, lx_ref[c, 8 * k : 8 * k + 8, lanes])], axis=0
                )
                stiff = jnp.concatenate([sx_ref[c, :, lanes]] * 6, axis=0)
                v = v_ref[c, :, lanes] + DT * (stiff * y - 0.5 * thick + load)
                v_ref[c, :, lanes] = v
                d_ref[c, :, lanes] = d + DT * v

    def substep(_, carry):
        split()
        update(slice(0, EXT), (slice(0, PTS), slice(PTS, EXT)))
        return carry

    lax.fori_loop(0, SUBSTEPS - 1, substep, 0)
    split()
    update(own, (own,))
    for c in range(N):
        if last:
            exponents = []
            for unit in range(6):
                rows = slice(16 * (unit % 3), 16 * (unit % 3) + 16)
                exponents.append(encode_rows(outs[0], c, unit, (d_ref, v_ref)[unit // 3][c, rows, own]))
            write_exponents(outs[0], c, exponents)
            continue
        for k in range(3):
            rows = slice(16 * k, 16 * k + 16)
            for ref, w in ((d_ref, 0), (v_ref, 1)):
                outs[0][c, w, k] = ref[c, rows, own]
                if not last:
                    halo = slice(48 * w + 16 * k, 48 * w + 16 * k + 16)
                    outs[1][c, halo, :] = ref[c, rows, HALO : 2 * HALO]
                    outs[2][c, halo, :] = ref[c, rows, PTS : PTS + HALO]
        if not last:
            static = st_ref[c]
            v_rows = jnp.concatenate([v_ref[c, 16 * k + 8 : 16 * k + 16, own] for k in range(3)], axis=0)
            speeds = patch_speeds(v_rows, static, node_onehot(static[6:7]))[4:8]
            outs[3][c] = speeds
            outs[4][c] = speeds.astype(BF16)


def solid(last, x, lo, hi, first_lo, first_hi, loading, load_lo, load_hi, static, matrices):


    whole = pl.BlockSpec(memory_space=pltpu.VMEM)

    def full(a):
        return pl.BlockSpec(a.shape, lambda i: (0,) * a.ndim)

    halo = full(lo)
    stiff = pl.BlockSpec((N, 16, HALO), lambda i: (0, STATIC_AT // 16, 0))
    outs = [jax.ShapeDtypeStruct((N, FINAL, PTS), jnp.int16) if last else jax.ShapeDtypeStruct((N, 2, 3, 16, PTS), F32)]
    if not last:
        outs += [jax.ShapeDtypeStruct((N, 96, HALO), F32)] * 2
        outs += [jax.ShapeDtypeStruct((N, QL, PTS), F32), jax.ShapeDtypeStruct((N, QL, PTS), BF16)]
    return pl.pallas_call(
        functools.partial(solid_kernel, last),
        grid=(1,),
        in_specs=[full(x), halo, halo, stiff, stiff]
        + [full(a) for a in (loading, load_lo, load_hi, static, *matrices)],
        out_specs=[full(o) for o in outs],
        out_shape=outs,
        scratch_shapes=[
            pltpu.VMEM((N, 48, EXT), F32),
            pltpu.VMEM((N, 48, EXT), F32),
            pltpu.VMEM((N + 2, 96, EXT), BF16),
            pltpu.VMEM((N, 24, EXT), F32),
            pltpu.VMEM((N, 8, EXT), F32),
        ],
        compiler_params=params(36),
        name="solid_last" if last else "solid",
    )(x, lo, hi, first_lo, first_hi, loading, load_lo, load_hi, static, *matrices)


def exchange(blocks, axis):
    return lax.all_to_all(blocks, axis, split_axis=0, concat_axis=0, tiled=True)


def copies(array, axis):
    return exchange(jnp.broadcast_to(array, (N, *array.shape)), axis)


def from_neighbours(first_rows, last_rows):
    down = [(i, i + 1) for i in range(N - 1)]
    up = [(b, a) for a, b in down]
    return lax.ppermute(last_rows, ROWS, down), lax.ppermute(first_rows, ROWS, up)


def on_device(displacement, velocity, stiffness, wet_position, wet_normal, wet_area, wet_map):
    shape = displacement.shape
    map_row = wet_map.astype(F32)[None]
    static_own = jnp.concatenate([wet_position, wet_normal, map_row, stiffness.reshape(1, PTS)], axis=0)
    source_own = jnp.concatenate([wet_position, wet_normal, wet_area[None], wet_area[None]], axis=0)
    static = copies(static_own, "tcol")
    coded, source = pack(
        displacement.reshape(3, PTS, PTS), velocity.reshape(3, PTS, PTS), static_own, source_own
    )
    static, source = lax.optimization_barrier((static, source))
    src = copies(source, ROWS)
    src, coded = lax.optimization_barrier((src, coded))
    x = exchange(coded, "tcol")
    kernel, partial = build(src, static)
    x, partial = lax.optimization_barrier((x, partial))
    x_first, x_last = x[:, :, :HALO], x[:, :, PTS - HALO :]
    lo, hi = from_neighbours(x_first, x_last)
    first_lo, first_hi = lo, hi
    speeds = first(x, static)
    matrices = tuple(jnp.asarray(m, BF16) for m in stencil_matrices())
    for repeat in range(COUPLED):
        received = exchange(partial, "tcol")
        loading, load_first, load_last = loads(received, speeds, static)
        load_lo, load_hi = from_neighbours(load_first, load_last)
        last = repeat == COUPLED - 1
        x, *more = solid(last, x, lo, hi, first_lo, first_hi, loading, load_lo, load_hi, static, matrices)
        if last:
            break
        x_first, x_last, speeds, rounded = more
        own = exchange(rounded, "tcol").reshape(LOADS, PTS)
        gathered = copies(own, ROWS)
        partial = product(kernel, gathered)
        partial, x_first = lax.optimization_barrier((partial, x_first))
        lo, hi = from_neighbours(x_first, x_last)
    d, v = unpack(exchange(x, "tcol"))
    return d.reshape(shape), v.reshape(shape)


def solution(mesh):
    state = P(None, ("group", "trow"), "tcol", None)
    points = P(("group", "trow", "tcol"))
    vectors = P(None, ("group", "trow", "tcol"))
    return jax.shard_map(
        on_device,
        mesh=mesh,
        in_specs=(state, state, P(("group", "trow"), "tcol"), vectors, vectors, points, points),
        out_specs=(state, state),
        check_vma=False,
    )
```

```python
import functools
import math

import jax
import jax.numpy as jnp
import numpy as np
from jax import lax
from jax.experimental import pallas as pl
from jax.experimental.pallas import tpu as pltpu
from jax.sharding import PartitionSpec as P

SUBSTEPS = 4
COUPLED = 2
N = 16
PTS = 256
PB = 8
LOADS = 64
SRC = LOADS + 24
QL = 4
HALO = 128
EXT = PTS + 2 * HALO
DT = 0.3
ROWS = ("group", "trow")
F32, BF16 = jnp.float32, jnp.bfloat16


def params(mib):
    return pltpu.CompilerParams(vmem_limit_bytes=mib << 20)


def split3(x):
    hi = x.astype(BF16).astype(F32)
    rest = x - hi
    mid = rest.astype(BF16).astype(F32)
    return hi, mid, (rest - mid).astype(BF16).astype(F32)


def encode(x):
    top = jnp.max(jnp.max(jnp.abs(x), axis=0, keepdims=True), axis=1, keepdims=True)
    exponent = jnp.floor(jnp.log2(jnp.maximum(top, 1e-30))) + 1.0
    scaled = jnp.round(x * jnp.exp2(15.0 - exponent))
    return jnp.clip(scaled, -32767.0, 32767.0), exponent


def to_i16(x):
    return x.astype(jnp.int32).astype(jnp.int16)


def from_i16(x):
    return x.astype(jnp.int32).astype(F32)


def encode_rows(ref, c, unit, x):
    values, exponent = encode(x)
    ref[c, 16 * unit : 16 * unit + 16, :] = to_i16(values)
    return jnp.broadcast_to(exponent, (1, PTS))


def write_exponents(ref, c, rows):
    ref[c, 96:104, :] = to_i16(jnp.concatenate(rows + rows[:2], axis=0))


def decode_scales(ref, c):
    return jnp.exp2(from_i16(ref[c, 96:104, :]) - 15.0)


def decode_rows(ref, c, unit, scales):
    return from_i16(ref[c, 16 * unit : 16 * unit + 16, :]) * scales[unit : unit + 1]


def pick_rows(values, onehot):
    rows = values.shape[0]
    parts = jnp.concatenate(split3(values), axis=0).astype(BF16)
    out = jnp.dot(parts, onehot, preferred_element_type=F32)
    return out[:rows] + out[rows : 2 * rows] + out[2 * rows :]


def node_onehot(map_row):
    nodes = lax.broadcasted_iota(jnp.int32, (PTS, PTS), 0).astype(F32)
    return jnp.where(nodes == map_row, 1.0, 0.0).astype(BF16)


FINAL = 104
STATIC_AT = 112
CODED = 128


def static_scale():
    row = lax.broadcasted_iota(jnp.int32, (8, PTS), 0)
    return jnp.where(row < 6, 4096.0, jnp.where(row == 6, 128.0, 2048.0))


def encode_static(rows):
    scaled = rows * static_scale()
    high = jnp.round(scaled)
    return jnp.concatenate([high, jnp.round((scaled - high) * 32768.0)], axis=0)


def decode_static(block):
    x = from_i16(block)
    scale = static_scale()[:, : block.shape[-1]]
    return (x[:8] + x[8:] * (1.0 / 32768.0)) * (1.0 / scale)


def pack_kernel(d_ref, v_ref, st_ref, so_ref, x_ref, sp_ref):
    exponents = [[] for _ in range(N)]
    speeds = None
    onehot = node_onehot(st_ref[6:7])
    for unit in range(6):
        k = unit % 3
        t = (d_ref, v_ref)[unit // 3][k].T
        for c in range(N):
            rows = [t[l * LOADS + c * QL : l * LOADS + (c + 1) * QL] for l in range(4)]
            exponents[c].append(encode_rows(x_ref, c, unit, jnp.concatenate(rows, axis=0)))
        if unit >= 3:
            term = pick_rows(t[3 * LOADS :], onehot) * st_ref[3 + k : 4 + k]
            speeds = term if speeds is None else speeds + term
    static = to_i16(encode_static(st_ref[...]))
    for c in range(N):
        write_exponents(x_ref, c, exponents[c])
        x_ref[c, 104:STATIC_AT, :] = jnp.zeros((8, PTS), jnp.int16)
        x_ref[c, STATIC_AT:, :] = static
    geometry = list(split3(so_ref[...]))
    sp_ref[...] = jnp.concatenate([speeds] + geometry, axis=0).astype(BF16)


def pack(d, v, static, source):
    return pl.pallas_call(
        pack_kernel,
        out_shape=[
            jax.ShapeDtypeStruct((N, CODED, PTS), jnp.int16),
            jax.ShapeDtypeStruct((SRC, PTS), BF16),
        ],
        compiler_params=params(16),
        name="pack",
    )(d, v, static, source)


def unpack_kernel(x_ref, d_ref, v_ref, t_ref):
    for c in range(N):
        scales = decode_scales(x_ref, c)
        for unit in range(6):
            rows = decode_rows(x_ref, c, unit, scales)
            for l in range(4):
                at = slice(l * LOADS + c * QL, l * LOADS + (c + 1) * QL)
                t_ref[unit, at, :] = rows[l * QL : (l + 1) * QL]
    for k in range(3):
        d_ref[k] = t_ref[k].T
        v_ref[k] = t_ref[3 + k].T


def unpack(x):
    return pl.pallas_call(
        unpack_kernel,
        out_shape=[jax.ShapeDtypeStruct((3, PTS, PTS), F32)] * 2,
        scratch_shapes=[pltpu.VMEM((6, PTS, PTS), F32)],
        compiler_params=params(16),
        name="unpack",
    )(x)


def feature_rows(parts, order, extra):
    rows = [parts[o] for o in order] + extra
    count = sum(r.shape[0] for r in rows)
    return jnp.concatenate(rows + [jnp.zeros((32 - count, rows[0].shape[1]), F32)], axis=0)


def squared(x):
    return jnp.sum(x * x, axis=0, keepdims=True)


SOURCE_ORDER = (0, 0, 0, 1, 1, 2)
TARGET_ORDER = (0, 1, 2, 0, 1, 0)
TB = 512


def build_kernel(src_ref, tgt_ref, k_ref, o_ref, fn_ref, fs_ref, sp_ref, mid_ref, e_ref):

    @pl.when(pl.program_id(0) == 0)
    def _():
        total = None
        for j in range(N):
            sp_ref[j * PTS : (j + 1) * PTS, :] = src_ref[j, :LOADS, :].T
            geometry = src_ref[j, LOADS:, :].astype(F32)
            geometry = geometry[:8] + geometry[8:16] + geometry[16:24]
            total = geometry if total is None else total + geometry
        mid_ref[...] = jnp.broadcast_to(jnp.sum(total, axis=1, keepdims=True) * (1.0 / (N * PTS)), (8, PTS))
        for j in range(N):
            geometry = src_ref[j, LOADS:, :].astype(F32)
            geometry = geometry[:8] + geometry[8:16] + geometry[16:24]
            p = geometry[:3] - mid_ref[:3, :]
            m = geometry[3:6] * (geometry[6:7] * (1.0 / (4.0 * math.pi)))
            shift = list(split3(-jnp.sum(m * p, axis=0, keepdims=True)))
            square = list(split3(squared(p) + 0.01))
            fn = feature_rows(split3(m), SOURCE_ORDER, shift)
            fs = feature_rows(split3(-2.0 * p), SOURCE_ORDER, square + [jnp.ones((3, PTS), F32)])
            at = slice(j * PTS, (j + 1) * PTS)
            fn_ref[:, at] = fn.astype(BF16)
            fs_ref[:, at] = fs.astype(BF16)

    for b in range(TB // PTS):
        t = tgt_ref[b, :3, :] - mid_ref[:3, :]
        ones = [jnp.ones((3, PTS), F32)]
        g = feature_rows(split3(t), TARGET_ORDER, ones + list(split3(squared(t)))).T.astype(BF16)
        for j in range(N):
            at = slice(j * PTS, (j + 1) * PTS)
            numerator = jnp.dot(g, fn_ref[:, at], preferred_element_type=F32)
            inverse = lax.rsqrt(jnp.dot(g, fs_ref[:, at], preferred_element_type=F32))
            k_ref[b * PTS : (b + 1) * PTS, at] = (numerator * inverse * (inverse * inverse)).astype(BF16)
    total = jnp.dot(k_ref[...], sp_ref[...], preferred_element_type=F32).T
    write_partial(total, o_ref, e_ref)


def write_partial(total, o_ref, e_ref):
    step = pl.program_id(0)
    width = total.shape[1]
    lane = lax.broadcasted_iota(jnp.int32, (LOADS, 128), 1)
    for b in range(width // TB):
        part = total[:, b * TB : (b + 1) * TB]
        top = jnp.max(jnp.abs(part), axis=1, keepdims=True)
        exponent = jnp.floor(jnp.log2(jnp.maximum(top, 1e-30))) + 1.0
        part = to_i16(jnp.clip(jnp.round(part * jnp.exp2(15.0 - exponent)), -32767.0, 32767.0))
        at = pl.ds(pl.multiple_of(step * width + b * TB, TB), TB)
        for c in range(N):
            o_ref[c, :, at] = part[c * QL : (c + 1) * QL]
        index = step * (width // TB) + b
        e_ref[...] = jnp.where(lane == index, exponent, jnp.where(index == 0, 0.0, e_ref[...]))

    @pl.when(step == pl.num_programs(0) - 1)
    def _():
        exponents = to_i16(e_ref[...])
        for c in range(N):
            o_ref[c, :, N * PTS :] = exponents[c * QL : (c + 1) * QL]


def build(src, tgt):
    points = N * PTS
    return pl.pallas_call(
        build_kernel,
        grid=(points // TB,),
        in_specs=[
            pl.BlockSpec((N, SRC, PTS), lambda i: (0, 0, 0)),
            pl.BlockSpec((TB // PTS, 8, PTS), lambda i: (i, 0, 0)),
        ],
        out_specs=[
            pl.BlockSpec((TB, points), lambda i: (i, 0)),
            pl.BlockSpec((N, QL, points + 128), lambda i: (0, 0, 0)),
        ],
        out_shape=[
            jax.ShapeDtypeStruct((points, points), BF16),
            jax.ShapeDtypeStruct((N, QL, points + 128), jnp.int16),
        ],
        scratch_shapes=[
            pltpu.VMEM((32, points), BF16),
            pltpu.VMEM((32, points), BF16),
            pltpu.VMEM((points, LOADS), BF16),
            pltpu.VMEM((8, PTS), F32),
            pltpu.VMEM((LOADS, 128), F32),
        ],
        compiler_params=params(24),
        cost_estimate=pl.CostEstimate(flops=20 << 30, bytes_accessed=100 << 20, transcendentals=16 << 20),
        name="build",
    )(src, tgt)


TB2 = 1024


def product_kernel(k_ref, own_ref, o_ref, sp_ref, e_ref):
    @pl.when(pl.program_id(0) == 0)
    def _():
        for j in range(N):
            sp_ref[j * PTS : (j + 1) * PTS, :] = own_ref[j].T

    total = jnp.dot(k_ref[...], sp_ref[...], preferred_element_type=F32).T
    write_partial(total, o_ref, e_ref)


def product(kernel, sp):
    points = N * PTS
    return pl.pallas_call(
        product_kernel,
        grid=(points // TB2,),
        in_specs=[
            pl.BlockSpec((TB2, points), lambda i: (i, 0)),
            pl.BlockSpec((N, LOADS, PTS), lambda i: (0, 0, 0)),
        ],
        out_specs=pl.BlockSpec((N, QL, points + 128), lambda i: (0, 0, 0)),
        out_shape=jax.ShapeDtypeStruct((N, QL, points + 128), jnp.int16),
        scratch_shapes=[pltpu.VMEM((points, LOADS), BF16), pltpu.VMEM((LOADS, 128), F32)],
        compiler_params=params(24),
        cost_estimate=pl.CostEstimate(flops=4 << 30, bytes_accessed=40 << 20, transcendentals=0),
        name="product",
    )(kernel, sp)


def patch_speeds(v_rows, static, onehot):
    picked = pick_rows(v_rows, onehot)
    return sum(static[3 + k : 4 + k] * picked[8 * k : 8 * k + 8] for k in range(3))


def first_kernel(x_ref, st_ref, s_ref):
    for c in range(N):
        static = st_ref[c]
        scales = decode_scales(x_ref, c)
        v_rows = jnp.concatenate([decode_rows(x_ref, c, 3 + k, scales)[8:] for k in range(3)], axis=0)
        s_ref[c] = patch_speeds(v_rows, static, node_onehot(static[6:7]))[4:8]


def first(x, static):
    return pl.pallas_call(
        first_kernel,
        out_shape=jax.ShapeDtypeStruct((N, QL, PTS), F32),
        compiler_params=params(20),
        name="first",
    )(x, static)


def load_kernel(rec_ref, s_ref, st_ref, l_ref, first_ref, last_ref):
    scales = [jnp.exp2(from_i16(rec_ref[j, :, N * PTS :]) - 15.0) for j in range(N)]
    for c in range(N):
        at = slice(c * PTS, (c + 1) * PTS)
        index = c * PTS // TB
        pressure = 0.5 * s_ref[c]
        for j in range(N):
            pressure = pressure + from_i16(rec_ref[j, :, at]) * scales[j][:, index : index + 1]
        pressure = jnp.concatenate([jnp.zeros_like(pressure), pressure], axis=0)
        static = st_ref[c]
        parts = jnp.concatenate([-(static[3 + k : 4 + k] * pressure) for k in range(3)], axis=0)
        parts = jnp.concatenate(split3(parts), axis=0).astype(BF16)
        out = lax.dot_general(
            parts, node_onehot(static[6:7]), (((1,), (1,)), ((), ())), preferred_element_type=F32
        )
        loading = out[:24] + out[24:48] + out[48:]
        l_ref[c] = loading
        for k in range(3):
            first_ref[c, k] = loading[8 * k + 4 : 8 * k + 8, :HALO]
            last_ref[c, k] = loading[8 * k + 4 : 8 * k + 8, PTS - HALO :]


def loads(rec, speeds, static):
    return pl.pallas_call(
        load_kernel,
        out_shape=[
            jax.ShapeDtypeStruct((N, 24, PTS), F32),
            jax.ShapeDtypeStruct((N, 3, QL, HALO), F32),
            jax.ShapeDtypeStruct((N, 3, QL, HALO), F32),
        ],
        compiler_params=params(20),
        name="loads",
    )(rec, speeds, static)


def stencil_matrices():
    taps = {0: -16.0, 1: 1.0, 2: 1.0, 3: 2.0}
    count = EXT // PB
    own = np.zeros((count, PB, count, PB), np.float32)
    left = np.zeros((PTS // PB, PB, PTS // PB, PB), np.float32)
    right = np.zeros_like(left)
    for a in range(count):
        for b in range(PB):
            own[a, b, a, b] = taps[0]
            for o in (1, 2, 3):
                for s in (o, -o):
                    if 0 <= a + s < count:
                        own[a + s, b, a, b] = taps[o]
                    if 0 <= b + s < PB:
                        own[a, b + s, a, b] = taps[o]
                    elif a < PTS // PB:
                        (left if s < 0 else right)[a, (b + s) % PB, a, b] = taps[o]
    return own.reshape(EXT, EXT), left.reshape(PTS, PTS), right.reshape(PTS, PTS)


GROUP = 2


def halo_stiffness(ref, c):
    return jnp.broadcast_to(decode_static(ref[c])[7:8] * (1.0 / 12.0), (8, HALO))


def solid_kernel(last, *refs):
    if last:
        x_ref, lo_ref, hi_ref, *refs = refs
    else:
        x_ref, lo_ref, hi_ref = coded = refs[:3]
        refs = refs[3:]
    slo_ref, shi_ref, l_ref, llo_ref, lhi_ref, st_ref, own_ref, left_ref, right_ref, *outs = refs
    *outs, d_ref, v_ref, xp_ref, lx_ref, sx_ref = outs
    own = slice(HALO, HALO + PTS)
    xp_ref[0] = jnp.zeros_like(xp_ref[0])
    xp_ref[N + 1] = jnp.zeros_like(xp_ref[0])
    for c in range(N):
        if not last:
            for source, at in zip(coded, (own, slice(0, HALO), slice(HALO + PTS, EXT))):
                scales = decode_scales(source, c)
                for unit in range(6):
                    rows = slice(16 * (unit % 3), 16 * (unit % 3) + 16)
                    (d_ref, v_ref)[unit // 3][c, rows, at] = decode_rows(source, c, unit, scales)
        for k in range(3):
            rows = slice(16 * k, 16 * k + 16)
            for ref, w in ((d_ref, 0), (v_ref, 1)) if last else ():
                halo = slice(48 * w + 16 * k, 48 * w + 16 * k + 16)
                ref[c, rows, :HALO] = lo_ref[c, halo, :]
                ref[c, rows, own] = x_ref[c, w, k]
                ref[c, rows, HALO + PTS :] = hi_ref[c, halo, :]
            zero = jnp.zeros((4, HALO), F32)
            lx_ref[c, 8 * k : 8 * k + 8, :HALO] = jnp.concatenate([zero, llo_ref[c, k]], axis=0)
            lx_ref[c, 8 * k : 8 * k + 8, own] = l_ref[c, 8 * k : 8 * k + 8]
            lx_ref[c, 8 * k : 8 * k + 8, HALO + PTS :] = jnp.concatenate([zero, lhi_ref[c, k]], axis=0)
        sx_ref[c, :, :HALO] = halo_stiffness(slo_ref, c)
        sx_ref[c, :, own] = jnp.broadcast_to(st_ref[c, 7:8, :], (8, PTS)) * (1.0 / 12.0)
        sx_ref[c, :, HALO + PTS :] = halo_stiffness(shi_ref, c)
    layer = lax.rem(lax.broadcasted_iota(jnp.int32, (48, EXT), 0), 16)
    below_top, above_bottom = layer < 12, layer >= 4

    def split():
        for c in range(N):
            d = d_ref[c]
            hi = d.astype(BF16)
            xp_ref[c + 1, :48] = hi
            xp_ref[c + 1, 48:] = (d - hi.astype(F32)).astype(BF16)

    def update(lanes, halves):
        count = lanes.stop - lanes.start
        for g in range(0, N, GROUP):
            total = jnp.dot(
                xp_ref[g + 1 : g + 1 + GROUP].reshape(GROUP * 96, EXT),
                own_ref[:, lanes],
                preferred_element_type=F32,
            )
            left = xp_ref[g : g + GROUP].reshape(GROUP * 96, EXT)
            right = xp_ref[g + 2 : g + 2 + GROUP].reshape(GROUP * 96, EXT)
            side = [
                jnp.dot(left[:, at], left_ref[...], preferred_element_type=F32)
                + jnp.dot(right[:, at], right_ref[...], preferred_element_type=F32)
                for at in halves
            ]
            total = total + jnp.concatenate(side, axis=1)
            for i in range(GROUP):
                c = g + i
                y = total[96 * i : 96 * i + 48] + total[96 * i + 48 : 96 * i + 96]
                d = d_ref[c, :, lanes]
                thick = jnp.where(below_top[:, :count], d - pltpu.roll(d, 44, 0), 0.0) + jnp.where(
                    above_bottom[:, :count], d - pltpu.roll(d, 4, 0), 0.0
                )
                zero = jnp.zeros((8, count), F32)
                load = jnp.concatenate(
                    [a for k in range(3) for a in (zero, lx_ref[c, 8 * k : 8 * k + 8, lanes])], axis=0
                )
                stiff = jnp.concatenate([sx_ref[c, :, lanes]] * 6, axis=0)
                v = v_ref[c, :, lanes] + DT * (stiff * y - 0.5 * thick + load)
                v_ref[c, :, lanes] = v
                d_ref[c, :, lanes] = d + DT * v

    def substep(_, carry):
        split()
        update(slice(0, EXT), (slice(0, PTS), slice(PTS, EXT)))
        return carry

    lax.fori_loop(0, SUBSTEPS - 1, substep, 0)
    split()
    update(own, (own,))
    for c in range(N):
        if last:
            exponents = []
            for unit in range(6):
                rows = slice(16 * (unit % 3), 16 * (unit % 3) + 16)
                exponents.append(encode_rows(outs[0], c, unit, (d_ref, v_ref)[unit // 3][c, rows, own]))
            write_exponents(outs[0], c, exponents)
            continue
        for k in range(3):
            rows = slice(16 * k, 16 * k + 16)
            for ref, w in ((d_ref, 0), (v_ref, 1)):
                outs[0][c, w, k] = ref[c, rows, own]
        if not last:
            static = st_ref[c]
            v_rows = jnp.concatenate([v_ref[c, 16 * k + 8 : 16 * k + 16, own] for k in range(3)], axis=0)
            speeds = patch_speeds(v_rows, static, node_onehot(static[6:7]))[4:8]
            outs[1][c] = speeds
            outs[2][c] = speeds.astype(BF16)


def solid(last, x, lo, hi, first_lo, first_hi, loading, load_lo, load_hi, static, matrices):


    whole = pl.BlockSpec(memory_space=pltpu.VMEM)

    def full(a):
        return pl.BlockSpec(a.shape, lambda i: (0,) * a.ndim)

    halo = full(lo)
    stiff = pl.BlockSpec((N, 16, HALO), lambda i: (0, STATIC_AT // 16, 0))
    outs = [jax.ShapeDtypeStruct((N, FINAL, PTS), jnp.int16) if last else jax.ShapeDtypeStruct((N, 2, 3, 16, PTS), F32)]
    if not last:
        outs += [jax.ShapeDtypeStruct((N, QL, PTS), F32), jax.ShapeDtypeStruct((N, QL, PTS), BF16)]
    return pl.pallas_call(
        functools.partial(solid_kernel, last),
        grid=(1,),
        in_specs=[full(x), halo, halo, stiff, stiff]
        + [full(a) for a in (loading, load_lo, load_hi, static, *matrices)],
        out_specs=[full(o) for o in outs],
        out_shape=outs,
        scratch_shapes=[
            pltpu.VMEM((N, 48, EXT), F32),
            pltpu.VMEM((N, 48, EXT), F32),
            pltpu.VMEM((N + 2, 96, EXT), BF16),
            pltpu.VMEM((N, 24, EXT), F32),
            pltpu.VMEM((N, 8, EXT), F32),
        ],
        compiler_params=params(36),
        name="solid_last" if last else "solid",
    )(x, lo, hi, first_lo, first_hi, loading, load_lo, load_hi, static, *matrices)


def exchange(blocks, axis):
    return lax.all_to_all(blocks, axis, split_axis=0, concat_axis=0, tiled=True)


def copies(array, axis):
    return exchange(jnp.broadcast_to(array, (N, *array.shape)), axis)


def from_neighbours(first_rows, last_rows):
    down = [(i, i + 1) for i in range(N - 1)]
    up = [(b, a) for a, b in down]
    return lax.ppermute(last_rows, ROWS, down), lax.ppermute(first_rows, ROWS, up)


def on_device(displacement, velocity, stiffness, wet_position, wet_normal, wet_area, wet_map):
    shape = displacement.shape
    map_row = wet_map.astype(F32)[None]
    static_own = jnp.concatenate([wet_position, wet_normal, map_row, stiffness.reshape(1, PTS)], axis=0)
    source_own = jnp.concatenate([wet_position, wet_normal, wet_area[None], wet_area[None]], axis=0)
    static = copies(static_own, "tcol")
    coded, source = pack(
        displacement.reshape(3, PTS, PTS), velocity.reshape(3, PTS, PTS), static_own, source_own
    )
    static, source = lax.optimization_barrier((static, source))
    src = copies(source, ROWS)
    src, coded = lax.optimization_barrier((src, coded))
    x = exchange(coded, "tcol")
    kernel, partial = build(src, static)
    x, partial = lax.optimization_barrier((x, partial))
    x_first, x_last = x[:, :, :HALO], x[:, :, PTS - HALO :]
    lo, hi = from_neighbours(x_first, x_last)
    first_lo, first_hi = lo, hi
    speeds = first(x, static)
    matrices = tuple(jnp.asarray(m, BF16) for m in stencil_matrices())
    for repeat in range(COUPLED):
        received = exchange(partial, "tcol")
        loading, load_first, load_last = loads(received, speeds, static)
        load_lo, load_hi = from_neighbours(load_first, load_last)
        last = repeat == COUPLED - 1
        x, *more = solid(last, x, lo, hi, first_lo, first_hi, loading, load_lo, load_hi, static, matrices)
        if last:
            break
        speeds, rounded = more
        own = exchange(rounded, "tcol").reshape(LOADS, PTS)
        gathered = copies(own, ROWS)
        partial = product(kernel, gathered)
        partial, x = lax.optimization_barrier((partial, x))
        rows = x.reshape(N, 96, PTS)
        lo, hi = from_neighbours(rows[:, :, :HALO], rows[:, :, PTS - HALO :])
    d, v = unpack(exchange(x, "tcol"))
    return d.reshape(shape), v.reshape(shape)


def solution(mesh):
    state = P(None, ("group", "trow"), "tcol", None)
    points = P(("group", "trow", "tcol"))
    vectors = P(None, ("group", "trow", "tcol"))
    return jax.shard_map(
        on_device,
        mesh=mesh,
        in_specs=(state, state, P(("group", "trow"), "tcol"), vectors, vectors, points, points),
        out_specs=(state, state),
        check_vma=False,
    )
```

```python
import functools
import math

import jax
import jax.numpy as jnp
import numpy as np
from jax import lax
from jax.experimental import pallas as pl
from jax.experimental.pallas import tpu as pltpu
from jax.sharding import PartitionSpec as P

SUBSTEPS = 4
COUPLED = 2
N = 16
PTS = 256
PB = 8
LOADS = 64
SRC = LOADS + 24
QL = 4
HALO = 128
EXT = PTS + 2 * HALO
DT = 0.3
ROWS = ("group", "trow")
F32, BF16 = jnp.float32, jnp.bfloat16


def params(mib):
    return pltpu.CompilerParams(vmem_limit_bytes=mib << 20)


def split3(x):
    hi = x.astype(BF16).astype(F32)
    rest = x - hi
    mid = rest.astype(BF16).astype(F32)
    return hi, mid, (rest - mid).astype(BF16).astype(F32)


def encode(x):
    top = jnp.max(jnp.max(jnp.abs(x), axis=0, keepdims=True), axis=1, keepdims=True)
    exponent = jnp.floor(jnp.log2(jnp.maximum(top, 1e-30))) + 1.0
    scaled = jnp.round(x * jnp.exp2(15.0 - exponent))
    return jnp.clip(scaled, -32767.0, 32767.0), exponent


def to_i16(x):
    return x.astype(jnp.int32).astype(jnp.int16)


def from_i16(x):
    return x.astype(jnp.int32).astype(F32)


def encode_rows(ref, c, unit, x):
    values, exponent = encode(x)
    ref[c, 16 * unit : 16 * unit + 16, :] = to_i16(values)
    return jnp.broadcast_to(exponent, (1, PTS))


def write_exponents(ref, c, rows):
    ref[c, 96:104, :] = to_i16(jnp.concatenate(rows + rows[:2], axis=0))


def decode_scales(ref, c):
    return jnp.exp2(from_i16(ref[c, 96:104, :]) - 15.0)


def decode_rows(ref, c, unit, scales):
    return from_i16(ref[c, 16 * unit : 16 * unit + 16, :]) * scales[unit : unit + 1]


def pick_rows(values, onehot):
    rows = values.shape[0]
    parts = jnp.concatenate(split3(values), axis=0).astype(BF16)
    out = jnp.dot(parts, onehot, preferred_element_type=F32)
    return out[:rows] + out[rows : 2 * rows] + out[2 * rows :]


def node_onehot(map_row):
    nodes = lax.broadcasted_iota(jnp.int32, (PTS, PTS), 0).astype(F32)
    return jnp.where(nodes == map_row, 1.0, 0.0).astype(BF16)


FINAL = 104
STATIC_AT = 112
CODED = 128


def static_scale():
    row = lax.broadcasted_iota(jnp.int32, (8, PTS), 0)
    return jnp.where(row < 6, 4096.0, jnp.where(row == 6, 128.0, 2048.0))


def encode_static(rows):
    scaled = rows * static_scale()
    high = jnp.round(scaled)
    return jnp.concatenate([high, jnp.round((scaled - high) * 32768.0)], axis=0)


def decode_static(block):
    x = from_i16(block)
    scale = static_scale()[:, : block.shape[-1]]
    return (x[:8] + x[8:] * (1.0 / 32768.0)) * (1.0 / scale)


def pack_kernel(d_ref, v_ref, st_ref, so_ref, x_ref, sp_ref):
    exponents = [[] for _ in range(N)]
    speeds = None
    onehot = node_onehot(st_ref[6:7])
    for unit in range(6):
        k = unit % 3
        t = (d_ref, v_ref)[unit // 3][k].T
        for c in range(N):
            rows = [t[l * LOADS + c * QL : l * LOADS + (c + 1) * QL] for l in range(4)]
            exponents[c].append(encode_rows(x_ref, c, unit, jnp.concatenate(rows, axis=0)))
        if unit >= 3:
            term = pick_rows(t[3 * LOADS :], onehot) * st_ref[3 + k : 4 + k]
            speeds = term if speeds is None else speeds + term
    static = to_i16(encode_static(st_ref[...]))
    for c in range(N):
        write_exponents(x_ref, c, exponents[c])
        x_ref[c, 104:STATIC_AT, :] = jnp.zeros((8, PTS), jnp.int16)
        x_ref[c, STATIC_AT:, :] = static
    geometry = list(split3(so_ref[...]))
    sp_ref[...] = jnp.concatenate([speeds] + geometry, axis=0).astype(BF16)


def pack(d, v, static, source):
    return pl.pallas_call(
        pack_kernel,
        out_shape=[
            jax.ShapeDtypeStruct((N, CODED, PTS), jnp.int16),
            jax.ShapeDtypeStruct((SRC, PTS), BF16),
        ],
        compiler_params=params(16),
        name="pack",
    )(d, v, static, source)


def unpack_kernel(x_ref, d_ref, v_ref, t_ref):
    for c in range(N):
        scales = decode_scales(x_ref, c)
        for unit in range(6):
            rows = decode_rows(x_ref, c, unit, scales)
            for l in range(4):
                at = slice(l * LOADS + c * QL, l * LOADS + (c + 1) * QL)
                t_ref[unit, at, :] = rows[l * QL : (l + 1) * QL]
    for k in range(3):
        d_ref[k] = t_ref[k].T
        v_ref[k] = t_ref[3 + k].T


def unpack(x):
    return pl.pallas_call(
        unpack_kernel,
        out_shape=[jax.ShapeDtypeStruct((3, PTS, PTS), F32)] * 2,
        scratch_shapes=[pltpu.VMEM((6, PTS, PTS), F32)],
        compiler_params=params(16),
        name="unpack",
    )(x)


def feature_rows(parts, order, extra):
    rows = [parts[o] for o in order] + extra
    count = sum(r.shape[0] for r in rows)
    return jnp.concatenate(rows + [jnp.zeros((32 - count, rows[0].shape[1]), F32)], axis=0)


def squared(x):
    return jnp.sum(x * x, axis=0, keepdims=True)


SOURCE_ORDER = (0, 0, 0, 1, 1, 2)
TARGET_ORDER = (0, 1, 2, 0, 1, 0)
TB = 512


def build_kernel(src_ref, tgt_ref, k_ref, o_ref, fn_ref, fs_ref, sp_ref, mid_ref, acc_ref):

    @pl.when(pl.program_id(0) == 0)
    def _():
        total = None
        for j in range(N):
            sp_ref[j * PTS : (j + 1) * PTS, :] = src_ref[j, :LOADS, :].T
            geometry = src_ref[j, LOADS:, :].astype(F32)
            geometry = geometry[:8] + geometry[8:16] + geometry[16:24]
            total = geometry if total is None else total + geometry
        mid_ref[...] = jnp.broadcast_to(jnp.sum(total, axis=1, keepdims=True) * (1.0 / (N * PTS)), (8, PTS))
        for j in range(N):
            geometry = src_ref[j, LOADS:, :].astype(F32)
            geometry = geometry[:8] + geometry[8:16] + geometry[16:24]
            p = geometry[:3] - mid_ref[:3, :]
            m = geometry[3:6] * (geometry[6:7] * (1.0 / (4.0 * math.pi)))
            shift = list(split3(-jnp.sum(m * p, axis=0, keepdims=True)))
            square = list(split3(squared(p) + 0.01))
            fn = feature_rows(split3(m), SOURCE_ORDER, shift)
            fs = feature_rows(split3(-2.0 * p), SOURCE_ORDER, square + [jnp.ones((3, PTS), F32)])
            at = slice(j * PTS, (j + 1) * PTS)
            fn_ref[:, at] = fn.astype(BF16)
            fs_ref[:, at] = fs.astype(BF16)

    for b in range(TB // PTS):
        t = tgt_ref[b, :3, :] - mid_ref[:3, :]
        ones = [jnp.ones((3, PTS), F32)]
        g = feature_rows(split3(t), TARGET_ORDER, ones + list(split3(squared(t)))).T.astype(BF16)
        for j in range(N):
            at = slice(j * PTS, (j + 1) * PTS)
            numerator = jnp.dot(g, fn_ref[:, at], preferred_element_type=F32)
            inverse = lax.rsqrt(jnp.dot(g, fs_ref[:, at], preferred_element_type=F32))
            k_ref[b * PTS : (b + 1) * PTS, at] = (numerator * inverse * (inverse * inverse)).astype(BF16)
    step = pl.program_id(0)
    total = jnp.dot(k_ref[...], sp_ref[...], preferred_element_type=F32).T
    width = total.shape[1]
    acc_ref[:, pl.ds(pl.multiple_of(step * width, width), width)] = total

    @pl.when(step == pl.num_programs(0) - 1)
    def _():
        write_partial(acc_ref, o_ref)


def write_partial(acc_ref, o_ref):
    lane = lax.broadcasted_iota(jnp.int32, (LOADS, 128), 1)
    exponents = jnp.zeros((LOADS, 128), F32)
    for b in range(N * PTS // TB):
        at = slice(b * TB, (b + 1) * TB)
        part = acc_ref[:, at]
        top = jnp.max(jnp.abs(part), axis=1, keepdims=True)
        exponent = jnp.floor(jnp.log2(jnp.maximum(top, 1e-30))) + 1.0
        part = to_i16(jnp.clip(jnp.round(part * jnp.exp2(15.0 - exponent)), -32767.0, 32767.0))
        for c in range(N):
            o_ref[c, :, at] = part[c * QL : (c + 1) * QL]
        exponents = jnp.where(lane == b, exponent, exponents)
    exponents = to_i16(exponents)
    for c in range(N):
        o_ref[c, :, N * PTS :] = exponents[c * QL : (c + 1) * QL]


def build(src, tgt):
    points = N * PTS
    return pl.pallas_call(
        build_kernel,
        grid=(points // TB,),
        in_specs=[
            pl.BlockSpec((N, SRC, PTS), lambda i: (0, 0, 0)),
            pl.BlockSpec((TB // PTS, 8, PTS), lambda i: (i, 0, 0)),
        ],
        out_specs=[
            pl.BlockSpec((TB, points), lambda i: (i, 0)),
            pl.BlockSpec((N, QL, points + 128), lambda i: (0, 0, 0)),
        ],
        out_shape=[
            jax.ShapeDtypeStruct((points, points), BF16),
            jax.ShapeDtypeStruct((N, QL, points + 128), jnp.int16),
        ],
        scratch_shapes=[
            pltpu.VMEM((32, points), BF16),
            pltpu.VMEM((32, points), BF16),
            pltpu.VMEM((points, LOADS), BF16),
            pltpu.VMEM((8, PTS), F32),
            pltpu.VMEM((LOADS, points), F32),
        ],
        compiler_params=params(24),
        cost_estimate=pl.CostEstimate(flops=20 << 30, bytes_accessed=100 << 20, transcendentals=16 << 20),
        name="build",
    )(src, tgt)


TB2 = 1024


def product_kernel(k_ref, own_ref, o_ref, sp_ref, acc_ref):
    @pl.when(pl.program_id(0) == 0)
    def _():
        for j in range(N):
            sp_ref[j * PTS : (j + 1) * PTS, :] = own_ref[j].T

    step = pl.program_id(0)
    total = jnp.dot(k_ref[...], sp_ref[...], preferred_element_type=F32).T
    width = total.shape[1]
    acc_ref[:, pl.ds(pl.multiple_of(step * width, width), width)] = total

    @pl.when(step == pl.num_programs(0) - 1)
    def _():
        write_partial(acc_ref, o_ref)


def product(kernel, sp):
    points = N * PTS
    return pl.pallas_call(
        product_kernel,
        grid=(points // TB2,),
        in_specs=[
            pl.BlockSpec((TB2, points), lambda i: (i, 0)),
            pl.BlockSpec((N, LOADS, PTS), lambda i: (0, 0, 0)),
        ],
        out_specs=pl.BlockSpec((N, QL, points + 128), lambda i: (0, 0, 0)),
        out_shape=jax.ShapeDtypeStruct((N, QL, points + 128), jnp.int16),
        scratch_shapes=[pltpu.VMEM((points, LOADS), BF16), pltpu.VMEM((LOADS, points), F32)],
        compiler_params=params(24),
        cost_estimate=pl.CostEstimate(flops=4 << 30, bytes_accessed=40 << 20, transcendentals=0),
        name="product",
    )(kernel, sp)


def patch_speeds(v_rows, static, onehot):
    picked = pick_rows(v_rows, onehot)
    return sum(static[3 + k : 4 + k] * picked[8 * k : 8 * k + 8] for k in range(3))


def first_kernel(x_ref, st_ref, s_ref):
    for c in range(N):
        static = st_ref[c]
        scales = decode_scales(x_ref, c)
        v_rows = jnp.concatenate([decode_rows(x_ref, c, 3 + k, scales)[8:] for k in range(3)], axis=0)
        s_ref[c] = patch_speeds(v_rows, static, node_onehot(static[6:7]))[4:8]


def first(x, static):
    return pl.pallas_call(
        first_kernel,
        out_shape=jax.ShapeDtypeStruct((N, QL, PTS), F32),
        compiler_params=params(20),
        name="first",
    )(x, static)


def load_kernel(rec_ref, s_ref, st_ref, l_ref, first_ref, last_ref):
    scales = [jnp.exp2(from_i16(rec_ref[j, :, N * PTS :]) - 15.0) for j in range(N)]
    for c in range(N):
        at = slice(c * PTS, (c + 1) * PTS)
        index = c * PTS // TB
        pressure = 0.5 * s_ref[c]
        for j in range(N):
            pressure = pressure + from_i16(rec_ref[j, :, at]) * scales[j][:, index : index + 1]
        pressure = jnp.concatenate([jnp.zeros_like(pressure), pressure], axis=0)
        static = st_ref[c]
        parts = jnp.concatenate([-(static[3 + k : 4 + k] * pressure) for k in range(3)], axis=0)
        parts = jnp.concatenate(split3(parts), axis=0).astype(BF16)
        out = lax.dot_general(
            parts, node_onehot(static[6:7]), (((1,), (1,)), ((), ())), preferred_element_type=F32
        )
        loading = out[:24] + out[24:48] + out[48:]
        l_ref[c] = loading
        for k in range(3):
            first_ref[c, k] = loading[8 * k + 4 : 8 * k + 8, :HALO]
            last_ref[c, k] = loading[8 * k + 4 : 8 * k + 8, PTS - HALO :]


def loads(rec, speeds, static):
    return pl.pallas_call(
        load_kernel,
        out_shape=[
            jax.ShapeDtypeStruct((N, 24, PTS), F32),
            jax.ShapeDtypeStruct((N, 3, QL, HALO), F32),
            jax.ShapeDtypeStruct((N, 3, QL, HALO), F32),
        ],
        compiler_params=params(20),
        name="loads",
    )(rec, speeds, static)


def stencil_matrices():
    taps = {0: -16.0, 1: 1.0, 2: 1.0, 3: 2.0}
    count = EXT // PB
    own = np.zeros((count, PB, count, PB), np.float32)
    left = np.zeros((PTS // PB, PB, PTS // PB, PB), np.float32)
    right = np.zeros_like(left)
    for a in range(count):
        for b in range(PB):
            own[a, b, a, b] = taps[0]
            for o in (1, 2, 3):
                for s in (o, -o):
                    if 0 <= a + s < count:
                        own[a + s, b, a, b] = taps[o]
                    if 0 <= b + s < PB:
                        own[a, b + s, a, b] = taps[o]
                    elif a < PTS // PB:
                        (left if s < 0 else right)[a, (b + s) % PB, a, b] = taps[o]
    return own.reshape(EXT, EXT), (left + right).reshape(PTS, PTS)


GROUP = 2


def halo_stiffness(ref, c):
    return jnp.broadcast_to(decode_static(ref[c])[7:8] * (1.0 / 12.0), (8, HALO))


def solid_kernel(last, *refs):
    if last:
        x_ref, lo_ref, hi_ref, *refs = refs
    else:
        x_ref, lo_ref, hi_ref = coded = refs[:3]
        refs = refs[3:]
    slo_ref, shi_ref, l_ref, llo_ref, lhi_ref, st_ref, own_ref, side_ref, *outs = refs
    *outs, d_ref, v_ref, xp_ref, xs_ref, lx_ref, sx_ref = outs
    own = slice(HALO, HALO + PTS)
    for c in range(N):
        if not last:
            for source, at in zip(coded, (own, slice(0, HALO), slice(HALO + PTS, EXT))):
                scales = decode_scales(source, c)
                for unit in range(6):
                    rows = slice(16 * (unit % 3), 16 * (unit % 3) + 16)
                    (d_ref, v_ref)[unit // 3][c, rows, at] = decode_rows(source, c, unit, scales)
        for k in range(3):
            rows = slice(16 * k, 16 * k + 16)
            for ref, w in ((d_ref, 0), (v_ref, 1)) if last else ():
                halo = slice(48 * w + 16 * k, 48 * w + 16 * k + 16)
                ref[c, rows, :HALO] = lo_ref[c, halo, :]
                ref[c, rows, own] = x_ref[c, w, k]
                ref[c, rows, HALO + PTS :] = hi_ref[c, halo, :]
            zero = jnp.zeros((4, HALO), F32)
            lx_ref[c, 8 * k : 8 * k + 8, :HALO] = jnp.concatenate([zero, llo_ref[c, k]], axis=0)
            lx_ref[c, 8 * k : 8 * k + 8, own] = l_ref[c, 8 * k : 8 * k + 8]
            lx_ref[c, 8 * k : 8 * k + 8, HALO + PTS :] = jnp.concatenate([zero, lhi_ref[c, k]], axis=0)
        sx_ref[c, :, :HALO] = halo_stiffness(slo_ref, c)
        sx_ref[c, :, own] = jnp.broadcast_to(st_ref[c, 7:8, :], (8, PTS)) * (1.0 / 12.0)
        sx_ref[c, :, HALO + PTS :] = halo_stiffness(shi_ref, c)
    layer = lax.rem(lax.broadcasted_iota(jnp.int32, (48, EXT), 0), 16)
    below_top, above_bottom = layer < 12, layer >= 4

    from_right = lax.rem(lax.broadcasted_iota(jnp.int32, (48, EXT), 1), PB) < PB // 2

    def write_split(ref, c, d):
        hi = d.astype(BF16)
        ref[c, :48] = hi
        ref[c, 48:] = (d - hi.astype(F32)).astype(BF16)

    def split():
        zero = jnp.zeros((48, EXT), F32)
        for c in range(N):
            write_split(xp_ref, c, d_ref[c])
            right = d_ref[c + 1] if c + 1 < N else zero
            left = d_ref[c - 1] if c > 0 else zero
            write_split(xs_ref, c, jnp.where(from_right, right, left))

    def update(lanes, halves):
        count = lanes.stop - lanes.start
        for g in range(0, N, GROUP):
            own_rows = xp_ref[g : g + GROUP].reshape(GROUP * 96, EXT)
            side_rows = xs_ref[g : g + GROUP].reshape(GROUP * 96, EXT)
            total = jnp.dot(own_rows, own_ref[:, lanes], preferred_element_type=F32)
            side = [jnp.dot(side_rows[:, at], side_ref[...], preferred_element_type=F32) for at in halves]
            total = total + jnp.concatenate(side, axis=1)
            for i in range(GROUP):
                c = g + i
                y = total[96 * i : 96 * i + 48] + total[96 * i + 48 : 96 * i + 96]
                d = d_ref[c, :, lanes]
                thick = jnp.where(below_top[:, :count], d - pltpu.roll(d, 44, 0), 0.0) + jnp.where(
                    above_bottom[:, :count], d - pltpu.roll(d, 4, 0), 0.0
                )
                zero = jnp.zeros((8, count), F32)
                load = jnp.concatenate(
                    [a for k in range(3) for a in (zero, lx_ref[c, 8 * k : 8 * k + 8, lanes])], axis=0
                )
                stiff = jnp.concatenate([sx_ref[c, :, lanes]] * 6, axis=0)
                v = v_ref[c, :, lanes] + DT * (stiff * y - 0.5 * thick + load)
                v_ref[c, :, lanes] = v
                d_ref[c, :, lanes] = d + DT * v

    def substep(_, carry):
        split()
        update(slice(0, EXT), (slice(0, PTS), slice(PTS, EXT)))
        return carry

    lax.fori_loop(0, SUBSTEPS - 1, substep, 0)
    split()
    update(own, (own,))
    for c in range(N):
        if last:
            exponents = []
            for unit in range(6):
                rows = slice(16 * (unit % 3), 16 * (unit % 3) + 16)
                exponents.append(encode_rows(outs[0], c, unit, (d_ref, v_ref)[unit // 3][c, rows, own]))
            write_exponents(outs[0], c, exponents)
            continue
        for k in range(3):
            rows = slice(16 * k, 16 * k + 16)
            for ref, w in ((d_ref, 0), (v_ref, 1)):
                outs[0][c, w, k] = ref[c, rows, own]
        if not last:
            static = st_ref[c]
            v_rows = jnp.concatenate([v_ref[c, 16 * k + 8 : 16 * k + 16, own] for k in range(3)], axis=0)
            speeds = patch_speeds(v_rows, static, node_onehot(static[6:7]))[4:8]
            outs[1][c] = speeds
            outs[2][c] = speeds.astype(BF16)


def solid(last, x, lo, hi, first_lo, first_hi, loading, load_lo, load_hi, static, matrices):


    whole = pl.BlockSpec(memory_space=pltpu.VMEM)

    def full(a):
        return pl.BlockSpec(a.shape, lambda i: (0,) * a.ndim)

    halo = full(lo)
    stiff = pl.BlockSpec((N, 16, HALO), lambda i: (0, STATIC_AT // 16, 0))
    outs = [jax.ShapeDtypeStruct((N, FINAL, PTS), jnp.int16) if last else jax.ShapeDtypeStruct((N, 2, 3, 16, PTS), F32)]
    if not last:
        outs += [jax.ShapeDtypeStruct((N, QL, PTS), F32), jax.ShapeDtypeStruct((N, QL, PTS), BF16)]
    return pl.pallas_call(
        functools.partial(solid_kernel, last),
        grid=(1,),
        in_specs=[full(x), halo, halo, stiff, stiff]
        + [full(a) for a in (loading, load_lo, load_hi, static, *matrices)],
        out_specs=[full(o) for o in outs],
        out_shape=outs,
        scratch_shapes=[
            pltpu.VMEM((N, 48, EXT), F32),
            pltpu.VMEM((N, 48, EXT), F32),
            pltpu.VMEM((N, 96, EXT), BF16),
            pltpu.VMEM((N, 96, EXT), BF16),
            pltpu.VMEM((N, 24, EXT), F32),
            pltpu.VMEM((N, 8, EXT), F32),
        ],
        compiler_params=params(36),
        name="solid_last" if last else "solid",
    )(x, lo, hi, first_lo, first_hi, loading, load_lo, load_hi, static, *matrices)


def exchange(blocks, axis):
    return lax.all_to_all(blocks, axis, split_axis=0, concat_axis=0, tiled=True)


def copies(array, axis):
    return exchange(jnp.broadcast_to(array, (N, *array.shape)), axis)


def from_neighbours(first_rows, last_rows):
    down = [(i, i + 1) for i in range(N - 1)]
    up = [(b, a) for a, b in down]
    return lax.ppermute(last_rows, ROWS, down), lax.ppermute(first_rows, ROWS, up)


def on_device(displacement, velocity, stiffness, wet_position, wet_normal, wet_area, wet_map):
    shape = displacement.shape
    map_row = wet_map.astype(F32)[None]
    static_own = jnp.concatenate([wet_position, wet_normal, map_row, stiffness.reshape(1, PTS)], axis=0)
    source_own = jnp.concatenate([wet_position, wet_normal, wet_area[None], wet_area[None]], axis=0)
    static = copies(static_own, "tcol")
    coded, source = pack(
        displacement.reshape(3, PTS, PTS), velocity.reshape(3, PTS, PTS), static_own, source_own
    )
    static, source = lax.optimization_barrier((static, source))
    src = copies(source, ROWS)
    src, coded = lax.optimization_barrier((src, coded))
    x = exchange(coded, "tcol")
    kernel, partial = build(src, static)
    x, partial = lax.optimization_barrier((x, partial))
    x_first, x_last = x[:, :, :HALO], x[:, :, PTS - HALO :]
    lo, hi = from_neighbours(x_first, x_last)
    first_lo, first_hi = lo, hi
    speeds = first(x, static)
    matrices = tuple(jnp.asarray(m, BF16) for m in stencil_matrices())
    for repeat in range(COUPLED):
        received = exchange(partial, "tcol")
        loading, load_first, load_last = loads(received, speeds, static)
        load_lo, load_hi = from_neighbours(load_first, load_last)
        last = repeat == COUPLED - 1
        x, *more = solid(last, x, lo, hi, first_lo, first_hi, loading, load_lo, load_hi, static, matrices)
        if last:
            break
        speeds, rounded = more
        own = exchange(rounded, "tcol").reshape(LOADS, PTS)
        gathered = copies(own, ROWS)
        partial = product(kernel, gathered)
        partial, x = lax.optimization_barrier((partial, x))
        rows = x.reshape(N, 96, PTS)
        lo, hi = from_neighbours(rows[:, :, :HALO], rows[:, :, PTS - HALO :])
    d, v = unpack(exchange(x, "tcol"))
    return d.reshape(shape), v.reshape(shape)


def solution(mesh):
    state = P(None, ("group", "trow"), "tcol", None)
    points = P(("group", "trow", "tcol"))
    vectors = P(None, ("group", "trow", "tcol"))
    return jax.shard_map(
        on_device,
        mesh=mesh,
        in_specs=(state, state, P(("group", "trow"), "tcol"), vectors, vectors, points, points),
        out_specs=(state, state),
        check_vma=False,
    )
```
